32 devices in a mesh: dp: 4 (over y, x), expert: 8 (over z, core).
Axes of the slice: x: 2, y: 2, z: 4, core: 2. Of those that a mesh axis runs over, the one named last changes fastest.
Arguments:
- tokens: bfloat16 [1024, 3584], P('expert', 'dp'), may hold values from -6 to 6
- expert_ids: int32 [1024, 8], P('expert'), may hold values from 0 to 7, as said below
- replica_choice: int32 [1024, 8], P('expert'), may hold values from 0 to 1, as said below
- gate_weights: float32 [1024, 8], P('expert'), may hold values from 0.1 to 1
- placement: int32 [4, 2], replicated, may hold values from 0 to 7, as said below
- capacity: int32 [12], replicated, may hold values from 16 to 32, as said below
- w_gate: bfloat16 [8, 2, 3584, 1024], P('expert', None, 'dp'), as said below
- w_up: bfloat16 [8, 2, 3584, 1024], P('expert', None, 'dp'), as said below
- w_down: bfloat16 [8, 2, 1024, 3584], P('expert', None, None, 'dp'), as said below
Outputs:
- combined: bfloat16 [1024, 3584], P('expert', 'dp')
The draws below stay inside these ranges and needn't reach their ends.
Inputs may be any that keep to these rules, and one draw needn't show every extreme that they name: `expert_ids`: each row names 8 different experts; in every aligned block of 128 rows some hot expert is named by at least 64 rows. `replica_choice`: 1 only where the slot's expert is hot; in every aligned block of 128 rows both replicas of some hot expert whose replicas have capacity 32 receive 32 or more slots. `placement`: column 0 holds 4 different expert numbers; column 1 holds 4 different expert-axis indices, none of them the own index of a hot expert. Entry e below 8 belongs to expert e's own replica, entry 8 + j to the copy of expert placement[j, 0]; both replicas of some hot expert have capacity 32. w_gate[placement[j, 1], 1] equals w_gate[placement[j, 0], 0]; entry [h, 1] is zero where index h hosts no copy. `w_up`: laid out as w_gate. `w_down`: laid out as w_gate.
All inputs are finite; a program needn't handle non-finite values.
Results may differ from the reference program's by a relative error of at most 0.0057.
Values may be sent and summed in bfloat16 or wider, within the bound.
No kernel may reach another device: no remote copies, remote signals or barrier semaphores. Data moves between devices by JAX's collectives and lax.ppermute only.
A program may use at most 128 MiB of HBM per device.

```python
import math
import jax
import jax.numpy as jnp
from jax import lax

D = 3584
FF = 1024
TOP = 8
TOK_DEV = 128
EXPERTS = 8
HOT = 4
CAP = 32
TOKENS = 1024


def routing_tables(key):
    base = jax.random.fold_in(key, 4242)
    keys = jax.random.split(base, 6)
    blocks = TOKENS // TOK_DEV
    expert_iota = jnp.arange(EXPERTS, dtype=jnp.int32)
    order = jax.random.permutation(keys[0], EXPERTS).astype(jnp.int32)
    hot_ids = order[:HOT]
    host_ids = order[HOT:2 * HOT]
    placement = jnp.stack([hot_ids, host_ids], 1).astype(jnp.int32)
    bias = jax.random.randint(keys[1], (EXPERTS,), 0, 4096, dtype=jnp.int32)
    noise = jax.random.randint(keys[2], (TOKENS, EXPERTS), 0, 4096, dtype=jnp.int32)
    tie = jax.random.randint(keys[3], (blocks, TOK_DEV), 0, 65536, dtype=jnp.int32)
    keyed = tie * TOK_DEV + jnp.arange(TOK_DEV, dtype=jnp.int32)[None, :]
    first = jnp.argsort(keyed, axis=1, stable=True)
    order_in = jnp.argsort(first, axis=1, stable=True).astype(jnp.int32).reshape(TOKENS)
    forced = order_in < 2 * CAP
    first_hot = hot_ids[0]
    boost = jnp.where(forced[:, None] & (expert_iota[None, :] == first_hot), 16384, 0)
    score = (noise + bias[None, :] + boost) * EXPERTS + expert_iota[None, :]
    _, chosen = lax.top_k(score, TOP)
    expert_ids = chosen.astype(jnp.int32)
    is_hot = jnp.any(expert_ids[:, :, None] == hot_ids[None, None, :], -1)
    coin = jax.random.randint(keys[4], (TOKENS, TOP), 0, 2, dtype=jnp.int32)
    replica = jnp.where(is_hot, coin, 0)
    first_slot = forced[:, None] & (jnp.arange(TOP, dtype=jnp.int32)[None, :] == 0)
    replica = jnp.where(first_slot, (order_in % 2)[:, None], replica).astype(jnp.int32)
    capacity = jax.random.randint(keys[5], (EXPERTS + HOT,), max(1, CAP // 2), CAP + 1, dtype=jnp.int32)
    entry_iota = jnp.arange(EXPERTS + HOT, dtype=jnp.int32)
    capacity = jnp.where((entry_iota == first_hot) | (entry_iota == EXPERTS), CAP, capacity).astype(jnp.int32)
    return (placement, expert_ids, replica, capacity)


def resident_weights(key, which, fan_in, rows, cols):
    placement = routing_tables(key)[0]
    base = jax.random.fold_in(key, 7100 + which)
    own = (jax.random.normal(base, (EXPERTS, rows, cols), jnp.float32) * fan_in ** (-0.5)).astype(jnp.bfloat16)
    device_iota = jnp.arange(EXPERTS, dtype=jnp.int32)
    guest_match = (placement[None, :, 1] == device_iota[:, None]).astype(jnp.int32)
    guest_expert = jnp.sum(guest_match * placement[None, :, 0], 1)
    has_guest = jnp.sum(guest_match, 1) > 0
    guest = jnp.where(has_guest[:, None, None], own[guest_expert], jnp.zeros((), jnp.bfloat16))
    return jnp.stack([own, guest], 1)


def draw_placement(key, part):
    return routing_tables(key)[0]


def draw_expert_ids(key, part):
    return routing_tables(key)[1]


def draw_replica_choice(key, part):
    return routing_tables(key)[2]


def draw_capacity(key, part):
    return routing_tables(key)[3]


def draw_w_gate(key, part):
    return resident_weights(key, 1, D, D, FF)


def draw_w_up(key, part):
    return resident_weights(key, 2, D, D, FF)


def draw_w_down(key, part):
    return resident_weights(key, 3, FF, FF, D)


def shard_levels(key, extent, shards, smallest, high):
    def one(axis_at, parts):
        heights = jax.random.uniform(jax.random.fold_in(jax.random.fold_in(key, 6), axis_at), (parts,), jnp.float32, smallest / len(shards), high / len(shards))
        return jnp.repeat(jnp.exp(heights), extent[axis_at] // parts).reshape((-1,) + (1,) * (len(extent) - axis_at - 1))

    level = one(*shards[0])
    for cut in shards[1:]:
        level = level * one(*cut)
    return level


def normal_values(key, extent, spread, bound, cuts=(), kind=jnp.bfloat16):
    drawn = spread * jax.random.normal(key, extent, jnp.float32)
    if cuts:
        drawn = drawn * shard_levels(key, extent, cuts, -0.22, 0.18)
    return jnp.clip(drawn, -bound, bound).astype(kind)


def setup_inputs(seed: int = 0) -> dict:
    seeds = jax.random.split(jax.random.key(seed), 10)
    return {
        "tokens": normal_values(seeds[0], (TOKENS, D), 1.0, 6.0, ((0, 8), (1, 4))),
        "expert_ids": draw_expert_ids(jax.random.fold_in(seeds[9], 71), 0),
        "replica_choice": draw_replica_choice(jax.random.fold_in(seeds[9], 71), 0),
        "gate_weights": jnp.clip(jnp.exp(math.log(1.0) - 2.3025851 * jax.random.uniform(seeds[3], (TOKENS, TOP), jnp.float32) ** shard_levels(seeds[3], (TOKENS, TOP), ((0, 8),), -0.2, 0.2)), 0.1, 1.0),
        "placement": draw_placement(jax.random.fold_in(seeds[9], 71), 0),
        "capacity": draw_capacity(jax.random.fold_in(seeds[9], 71), 0),
        "w_gate": draw_w_gate(jax.random.fold_in(seeds[9], 71), 0),
        "w_up": draw_w_up(jax.random.fold_in(seeds[9], 71), 0),
        "w_down": draw_w_down(jax.random.fold_in(seeds[9], 71), 0),
    }


def reference(tokens, expert_ids, replica_choice, gate_weights, placement, capacity, w_gate, w_up, w_down):
    blocks = TOKENS // TOK_DEV
    slot_count = TOK_DEV * TOP
    all_slots = TOKENS * TOP
    hot_ids = placement[:, 0]
    flat_ids = expert_ids.reshape(blocks, slot_count)
    flat_rep = replica_choice.reshape(blocks, slot_count)
    hot_match = (flat_ids[:, :, None] == hot_ids[None, None, :]).astype(jnp.int32)
    hot_slot = jnp.sum(hot_match * jnp.arange(HOT, dtype=jnp.int32)[None, None, :], -1)
    target = jnp.where(flat_rep == 1, EXPERTS + hot_slot, flat_ids)
    onehot = (target[:, :, None] == jnp.arange(EXPERTS + HOT, dtype=jnp.int32)[None, None, :]).astype(jnp.int32)
    before = jnp.cumsum(onehot, 1) - onehot
    slot_rank = jnp.sum(before * onehot, -1)
    slot_limit = jnp.sum(onehot * capacity[None, None, :], -1)
    retained = slot_rank < slot_limit
    per_expert = blocks * 2 * CAP
    block_index = jnp.arange(blocks, dtype=jnp.int32)[:, None]
    position = jnp.where(retained, flat_ids * per_expert + (block_index * 2 + flat_rep) * CAP + slot_rank, EXPERTS * per_expert).astype(jnp.int32)
    slot_ids = jnp.arange(all_slots, dtype=jnp.int32)
    table = jnp.full((EXPERTS * per_expert,), all_slots, jnp.int32)
    table = table.at[position.reshape(-1)].set(slot_ids, mode="drop").reshape(EXPERTS, per_expert)
    flat_weights = gate_weights.reshape(-1)

    def one_expert(combined, inputs):
        entries, gate_mat, up_mat, down_mat = inputs
        valid = entries < all_slots
        safe = jnp.minimum(entries, all_slots - 1).astype(jnp.int32)
        token_index = (safe // TOP).astype(jnp.int32)
        token_rows = jnp.where(valid[:, None], tokens[token_index], jnp.zeros((), tokens.dtype))
        gate_part = jnp.dot(token_rows, gate_mat, preferred_element_type=jnp.float32)
        up_part = jnp.dot(token_rows, up_mat, preferred_element_type=jnp.float32)
        hidden = (jax.nn.silu(gate_part) * up_part).astype(jnp.bfloat16)
        result = jnp.dot(hidden, down_mat, preferred_element_type=jnp.float32).astype(jnp.bfloat16)
        scale = jnp.where(valid, flat_weights[safe], jnp.zeros((), jnp.float32))
        combined = combined.at[token_index].add(scale[:, None] * result.astype(jnp.float32))
        return combined, None

    combined, _ = lax.scan(one_expert, jnp.zeros((TOKENS, D), jnp.float32), (table, w_gate[:, 0], w_up[:, 0], w_down[:, 0]))
    return combined.astype(jnp.bfloat16)
```

```python
import functools

import jax
import jax.numpy as jnp
from jax import lax
from jax.experimental import pallas as pl
from jax.experimental.pallas import tpu as pltpu
from jax.sharding import PartitionSpec as P

BF16 = jnp.bfloat16
F32 = jnp.float32
I32 = jnp.int32
DIRECT_LIMIT = 8


def round_up(n, m):
    return -(-n // m) * m


def slot_room(token_count, top_count, expert_count):
    return max(2, min(token_count // 4, 3 * token_count * top_count // (4 * expert_count)))


def dot(a, b):
    return jnp.dot(a, b, preferred_element_type=F32)


def vmem_specs(n):
    return [pl.BlockSpec(memory_space=pltpu.VMEM)] * n


SMEM_SPEC = pl.BlockSpec(memory_space=pltpu.SMEM)


def route_kernel(
    sizes, flip, place, cap, ids_ref, choice_ref, gate_ref, tok_ref, high_ref, low_ref, *out_refs
):
    experts, hot, room, half, room_a, room_b = sizes
    count, top = ids_ref.shape
    per = room_a + room_b
    columns = experts * per
    ids, choice, gate = ids_ref[...], choice_ref[...], gate_ref[...]
    lane = lax.broadcasted_iota(I32, (count, 2 * experts), 1)
    key = ids + experts * choice
    member = jnp.zeros((count, 2 * experts), F32)
    weight = jnp.zeros((count, 2 * experts), F32)
    for k in range(top):
        hit = key[:, k : k + 1] == lane
        member = jnp.where(hit, 1.0, member)
        weight = jnp.where(hit, gate[:, k : k + 1], weight)
    earlier = lax.broadcasted_iota(I32, (count, count), 1) < lax.broadcasted_iota(
        I32, (count, count), 0
    )
    rank = dot(jnp.where(earlier, 1.0, 0.0).astype(BF16), member.astype(BF16))
    lane_row = lax.broadcasted_iota(I32, (1, 2 * experts), 1)
    limit = jnp.zeros((1, 2 * experts), I32)
    for e in range(experts):
        limit = jnp.where(lane_row == e, cap[e], limit)
    for j in range(hot):
        limit = jnp.where(lane_row == place[j, 0] + experts, cap[experts + j], limit)
    kept = (member > 0.5) & (rank < limit.astype(F32))
    rank = jnp.where(kept, rank, -1.0)

    column = lax.broadcasted_iota(I32, (1, columns), 1)
    block = jnp.floor((column.astype(F32) + 0.5) * (1.0 / per)).astype(I32)
    slot = column - block * per
    dest = block ^ flip[0]
    pair_key = jnp.full((1, columns), -1, I32)
    start = jnp.zeros((1, columns), I32)
    for j in range(hot):
        owner, host = dest == place[j, 0], dest == place[j, 1]
        pair_key = jnp.where(owner | host, place[j, 0] + experts, pair_key)
        start = jnp.where(host, half, start)
    first = slot < room_a
    in_pair = slot - room_a
    wanted = jnp.where(first, dest, jnp.where(in_pair < half, pair_key, -1))
    place_rank = jnp.where(first, slot, in_pair + start).astype(F32)
    spread = jnp.where(
        lax.broadcasted_iota(I32, (2 * experts, columns), 0) == wanted, 1.0, 0.0
    ).astype(BF16)
    usable = jnp.max(spread.astype(F32), axis=0, keepdims=True) > 0.5
    chosen = (dot(rank.astype(BF16), spread) == place_rank) & usable
    weight_high = weight.astype(BF16)
    weight_low = (weight - weight_high.astype(F32)).astype(BF16)
    high_ref[...] = jnp.where(chosen, dot(weight_high, spread), 0.0).astype(BF16)
    low_ref[...] = jnp.where(chosen, dot(weight_low, spread), 0.0).astype(BF16)
    picks = jnp.where(chosen, 1.0, 0.0).T.astype(BF16)
    rows = dot(picks, tok_ref[...]).astype(BF16)
    for i, ref in enumerate(out_refs):
        ref[...] = rows[i * per : (i + 1) * per]


def up_kernel(sizes, at, *refs):
    experts, parts, room_a, room_b = sizes
    x_refs = refs[:experts]
    wg0, wg1, wu0, wu1 = refs[experts : experts + 4]
    outs = refs[experts + 4 : experts + 4 + parts]
    xa, xb, acc_a, acc_b = refs[experts + 4 + parts :]

    @pl.when(pl.program_id(0) == 0)
    def _():
        for i, ref in enumerate(x_refs):
            xa[i * room_a : (i + 1) * room_a] = ref[:room_a]
            xb[i * room_b : (i + 1) * room_b] = ref[room_a:]

    rows_a, rows_b = experts * room_a // parts, experts * room_b // parts
    for g, (first, second) in enumerate(((wg0, wg1), (wu0, wu1))):
        acc_a[...] = dot(xa[...], first[0, 0])
        acc_b[...] = dot(xb[...], second[0, 0])
        for k, out in enumerate(outs):
            q = at[0] ^ k
            out[g, :rows_a] = acc_a[pl.ds(q * rows_a, rows_a)].astype(out.dtype)
            out[g, rows_a:] = acc_b[pl.ds(q * rows_b, rows_b)].astype(out.dtype)


def hidden_kernel(own, *refs):
    out = refs[-1]
    total = own[...]
    for ref in refs[:-1]:
        total += ref[...].astype(F32)
    out[...] = (jax.nn.silu(total[0]) * total[1]).astype(BF16)


def down_kernel(sizes, at, *refs):
    experts, parts, room_a, room_b = sizes
    hids = refs[:parts]
    w0, w1 = refs[parts : parts + 2]
    outs = refs[parts + 2 : parts + 2 + experts]
    ha, hb = refs[parts + 2 + experts :]
    rows_a, rows_b = experts * room_a // parts, experts * room_b // parts
    for k, ref in enumerate(hids):
        q = at[0] ^ k
        ha[pl.ds(q * rows_a, rows_a)] = ref[:rows_a]
        hb[pl.ds(q * rows_b, rows_b)] = ref[rows_a:]
    ra = dot(ha[...], w0[0, 0]).astype(BF16)
    rb = dot(hb[...], w1[0, 0]).astype(BF16)
    for i, out in enumerate(outs):
        out[:room_a] = ra[i * room_a : (i + 1) * room_a]
        out[room_a:] = rb[i * room_b : (i + 1) * room_b]


def combine_kernel(high, low, *refs):
    out, res = refs[-2:]
    per = refs[0].shape[0]
    for i, ref in enumerate(refs[:-2]):
        res[i * per : (i + 1) * per] = ref[...]
    rows = res[...]
    out[...] = (dot(high[...], rows) + dot(low[...], rows)).astype(BF16)


def flips(n, j):
    return [(i, i ^ j) for i in range(n)]


def exchange(pieces, axis):
    n = len(pieces)
    if n <= DIRECT_LIMIT:
        return [pieces[0]] + [lax.ppermute(x, axis, flips(n, j)) for j, x in enumerate(pieces) if j]
    moved = lax.all_to_all(jnp.stack(pieces), axis, split_axis=0, concat_axis=0, tiled=True)
    return [moved[i] for i in range(n)]


def on_device(
    tokens, expert_ids, replica_choice, gate_weights, placement, capacity, w_gate, w_up, w_down
):
    experts = lax.axis_size("expert")
    parts = lax.axis_size("dp")
    me = lax.axis_index("expert")
    count, cols = tokens.shape
    ff = w_gate.shape[3]
    hot = placement.shape[0]
    room = slot_room(count, expert_ids.shape[1], experts)
    half = -(-room // 2)
    room_a, room_b = round_up(room, 16), round_up(half, 16)
    per = room_a + room_b
    direct = experts <= DIRECT_LIMIT
    flip = jnp.where(direct, me, 0).astype(I32).reshape(1)
    hosting = jnp.any(placement[:, 1] == me)
    second = hosting.astype(I32)
    at = lax.axis_index("dp").astype(I32).reshape(1)

    sds = jax.ShapeDtypeStruct
    high, low, *pieces = pl.pallas_call(
        functools.partial(route_kernel, (experts, hot, room, half, room_a, room_b)),
        out_shape=[sds((count, experts * per), BF16)] * 2 + [sds((per, cols), BF16)] * experts,
        in_specs=[SMEM_SPEC] * 3 + vmem_specs(4),
        out_specs=vmem_specs(2 + experts),
        name="route",
    )(flip, placement, capacity, expert_ids, replica_choice, gate_weights, tokens)
    arrived = exchange(pieces, "expert")

    block = 256 if ff % 256 == 0 else ff
    rows = experts * per // parts
    scalars = jnp.concatenate([at, second.reshape(1)])
    w_specs = [
        pl.BlockSpec((1, 1, cols, block), lambda f, s: (0, 0, 0, f)),
        pl.BlockSpec((1, 1, cols, block), lambda f, s: (0, s[1], 0, f)),
    ]
    sums = pl.pallas_call(
        functools.partial(up_kernel, (experts, parts, room_a, room_b)),
        out_shape=[sds((2, rows, ff), F32)] + [sds((2, rows, ff), BF16)] * (parts - 1),
        grid_spec=pltpu.PrefetchScalarGridSpec(
            num_scalar_prefetch=1,
            grid=(ff // block,),
            in_specs=[pl.BlockSpec((per, cols), lambda f, s: (0, 0))] * experts + w_specs * 2,
            out_specs=[pl.BlockSpec((2, rows, block), lambda f, s: (0, 0, f))] * parts,
            scratch_shapes=[
                pltpu.VMEM((experts * room_a, cols), BF16),
                pltpu.VMEM((experts * room_b, cols), BF16),
                pltpu.VMEM((experts * room_a, block), F32),
                pltpu.VMEM((experts * room_b, block), F32),
            ],
        ),
        name="gate_up",
    )(scalars, *arrived, w_gate, w_gate, w_up, w_up)
    sums = [sums[0]] + [lax.ppermute(x, "dp", flips(parts, j)) for j, x in enumerate(sums) if j]
    hidden = pl.pallas_call(
        hidden_kernel,
        out_shape=sds((rows, ff), BF16),
        in_specs=vmem_specs(parts),
        out_specs=vmem_specs(1)[0],
        name="hidden",
    )(*sums)
    spread = [hidden] + [lax.ppermute(hidden, "dp", flips(parts, j)) for j in range(1, parts)]
    results = pl.pallas_call(
        functools.partial(down_kernel, (experts, parts, room_a, room_b)),
        out_shape=[sds((per, cols), BF16)] * experts,
        grid_spec=pltpu.PrefetchScalarGridSpec(
            num_scalar_prefetch=1,
            grid=(1,),
            in_specs=[pl.BlockSpec((rows, ff), lambda f, s: (0, 0))] * parts
            + [
                pl.BlockSpec((1, 1, ff, cols), lambda f, s: (0, 0, 0, 0)),
                pl.BlockSpec((1, 1, ff, cols), lambda f, s: (0, s[1], 0, 0)),
            ],
            out_specs=[pl.BlockSpec((per, cols), lambda f, s: (0, 0))] * experts,
            scratch_shapes=[
                pltpu.VMEM((experts * room_a, ff), BF16),
                pltpu.VMEM((experts * room_b, ff), BF16),
            ],
        ),
        name="down",
    )(scalars, *spread, w_down, w_down)
    returned = exchange(results, "expert")
    return pl.pallas_call(
        combine_kernel,
        out_shape=sds((count, cols), BF16),
        in_specs=vmem_specs(2 + experts),
        out_specs=vmem_specs(1)[0],
        scratch_shapes=[pltpu.VMEM((experts * per, cols), BF16)],
        name="combine",
    )(high, low, *returned)


def solution(mesh):
    return jax.shard_map(
        on_device,
        mesh=mesh,
        in_specs=(
            P("expert", "dp"),
            P("expert", None),
            P("expert", None),
            P("expert", None),
            P(),
            P(),
            P("expert", None, "dp", None),
            P("expert", None, "dp", None),
            P("expert", None, None, "dp"),
        ),
        out_specs=P("expert", "dp"),
        check_vma=False,
    )
```

```python
import functools

import jax
import jax.numpy as jnp
from jax import lax
from jax.experimental import pallas as pl
from jax.experimental.pallas import tpu as pltpu
from jax.sharding import PartitionSpec as P


BF16 = jnp.bfloat16
F32 = jnp.float32
I32 = jnp.int32
DIRECT_LIMIT = 8


def round_up(n, m):
    return -(-n // m) * m


def slot_room(token_count, top_count, expert_count):
    return max(2, min(token_count // 4, 3 * token_count * top_count // (4 * expert_count)))


def dot(a, b):
    return jnp.dot(a, b, preferred_element_type=F32)


def vmem_specs(n):
    return [pl.BlockSpec(memory_space=pltpu.VMEM)] * n


PARAMS = pltpu.CompilerParams(vmem_limit_bytes=24 * 2**20)


def cost(flops, size):
    return pl.CostEstimate(flops=flops, bytes_accessed=size, transcendentals=0)


SMEM_SPEC = pl.BlockSpec(memory_space=pltpu.SMEM)


def route_kernel(
    sizes, here, place, cap, ids_ref, choice_ref, gate_ref, tok_ref, second, high_ref, low_ref,
    *out_refs
):
    experts, hot, _, half, room_a, room_b = sizes
    top, count = ids_ref.shape
    per = room_a + room_b
    columns = experts * per
    hosting = jnp.int32(0)
    for j in range(hot):
        hosting = jnp.where(place[1, j] == here[1], 1, hosting)
    second[0] = here[2]
    second[1] = hosting
    key = (ids_ref[...] + experts * choice_ref[...]).astype(F32).T
    gate = gate_ref[...].T
    lane = lax.broadcasted_iota(I32, (count, 2 * experts), 1).astype(F32)
    member = jnp.zeros((count, 2 * experts), F32)
    weight = jnp.zeros((count, 2 * experts), F32)
    for k in range(top):
        hit = key[:, k : k + 1] == lane
        member = jnp.where(hit, 1.0, member)
        weight = jnp.where(hit, gate[:, k : k + 1], weight)
    earlier = lax.broadcasted_iota(I32, (count, count), 1) < lax.broadcasted_iota(
        I32, (count, count), 0
    )
    rank = dot(jnp.where(earlier, 1.0, 0.0).astype(BF16), member.astype(BF16))
    lane_row = lax.broadcasted_iota(I32, (1, 2 * experts), 1)
    limit = jnp.zeros((1, 2 * experts), I32)
    for e in range(experts):
        limit = jnp.where(lane_row == e, cap[e], limit)
    for j in range(hot):
        limit = jnp.where(lane_row == place[0, j] + experts, cap[experts + j], limit)
    kept = (member > 0.5) & (rank < limit.astype(F32))
    rank = jnp.where(kept, rank, -1.0)

    column = lax.broadcasted_iota(I32, (1, columns), 1)
    block = jnp.floor((column.astype(F32) + 0.5) * (1.0 / per)).astype(I32)
    slot = column - block * per
    dest = block ^ here[0]
    pair_key = jnp.full((1, columns), -1, I32)
    start = jnp.zeros((1, columns), I32)
    for j in range(hot):
        owner, host = dest == place[0, j], dest == place[1, j]
        pair_key = jnp.where(owner | host, place[0, j] + experts, pair_key)
        start = jnp.where(host, half, start)
    first = slot < room_a
    in_pair = slot - room_a
    wanted = jnp.where(first, dest, jnp.where(in_pair < half, pair_key, -1))
    place_rank = jnp.where(first, slot, in_pair + start).astype(F32)
    spread = jnp.where(
        lax.broadcasted_iota(I32, (2 * experts, columns), 0) == wanted, 1.0, 0.0
    ).astype(BF16)
    chosen = (dot(rank.astype(BF16), spread) == place_rank) & (wanted >= 0)
    weight_high = weight.astype(BF16)
    weight_low = (weight - weight_high.astype(F32)).astype(BF16)
    high_ref[...] = jnp.where(chosen, dot(weight_high, spread), 0.0).astype(BF16)
    low_ref[...] = jnp.where(chosen, dot(weight_low, spread), 0.0).astype(BF16)
    picks = jnp.where(chosen, 1.0, 0.0).T.astype(BF16)
    rows = dot(picks, tok_ref[...]).astype(BF16)
    for i, ref in enumerate(out_refs):
        ref[...] = rows[i * per : (i + 1) * per]


def stage_kernel(at, w_gate, w_up, *refs):
    outs, sems = refs[:-1], refs[-1]
    block = outs[0].shape[2] // 2
    copies = []
    for k, out in enumerate(outs):
        columns = pl.ds(pl.multiple_of((at[0] ^ k) * block, block), block)
        for i, which in enumerate((0, at[1])):
            for g, w in enumerate((w_gate, w_up)):
                copies.append(
                    pltpu.make_async_copy(
                        w.at[0, which, :, columns],
                        out.at[i, :, pl.ds(g * block, block)],
                        sems.at[len(copies)],
                    )
                )
    for copy in copies:
        copy.start()
    for copy in copies:
        copy.wait()


def up_sums(xa, xb, weights, out):
    rows_a = xa.shape[0]
    out[:rows_a] = dot(xa, weights[0]).astype(out.dtype)
    out[rows_a:] = dot(xb, weights[1]).astype(out.dtype)


def up_first_kernel(sizes, *refs):
    experts, room_a, room_b = sizes
    x_refs, weights = refs[:experts], refs[experts]
    out, xa, xb = refs[experts + 1 :]
    for i, ref in enumerate(x_refs):
        xa[i * room_a : (i + 1) * room_a] = ref[:room_a]
        xb[i * room_b : (i + 1) * room_b] = ref[room_a:]
    up_sums(xa[...], xb[...], weights, out)


def up_next_kernel(xa, xb, weights, out):
    up_sums(xa[...], xb[...], weights, out)


def hidden_kernel(own, *refs):
    out = refs[-1]
    block = own.shape[1] // 2
    total = own[...]
    for ref in refs[:-1]:
        total += ref[...].astype(F32)
    out[...] = (jax.nn.silu(total[:, :block]) * total[:, block:]).astype(BF16)


def down_sums(hids, weights, rows_a):
    ra = sum(dot(h[:rows_a], w[0, 0]) for h, w in zip(hids, weights[0::2]))
    rb = sum(dot(h[rows_a:], w[0, 0]) for h, w in zip(hids, weights[1::2]))
    return ra, rb


def down_first_kernel(n, rows_a, at, *refs):
    out = refs[-1]
    out[:rows_a], out[rows_a:] = down_sums(refs[:n], refs[n:-1], rows_a)


def down_last_kernel(n, sizes, at, acc, *refs):
    experts, room_a, room_b = sizes
    rows_a = experts * room_a
    outs = refs[3 * n :]
    ra, rb = down_sums(refs[:n], refs[n : 3 * n], rows_a)
    ra = (ra + acc[:rows_a]).astype(BF16)
    rb = (rb + acc[rows_a:]).astype(BF16)
    for i, out in enumerate(outs):
        out[:room_a] = ra[i * room_a : (i + 1) * room_a]
        out[room_a:] = rb[i * room_b : (i + 1) * room_b]


def combine_kernel(high, low, *refs):
    out, res = refs[-2:]
    per = refs[0].shape[0]
    for i, ref in enumerate(refs[:-2]):
        res[i * per : (i + 1) * per] = ref[...]
    rows = res[...]
    out[...] = (dot(high[...], rows) + dot(low[...], rows)).astype(BF16)


def flips(n, j):
    return [(i, i ^ j) for i in range(n)]


def exchange(pieces, axis):
    n = len(pieces)
    if n > DIRECT_LIMIT:
        moved = lax.all_to_all(jnp.stack(pieces), axis, split_axis=0, concat_axis=0, tiled=True)
        return [moved[i] for i in range(n)]
    moved = [pieces[0]]
    for j in range(1, n):
        moved.append(lax.ppermute(pieces[j], axis, flips(n, j)))
    return moved


def on_device(
    tokens, expert_ids, replica_choice, gate_weights, placement, capacity, w_gate, w_up, w_down
):
    experts = lax.axis_size("expert")
    parts = lax.axis_size("dp")
    me = lax.axis_index("expert").astype(I32)
    count, cols = tokens.shape
    ff = w_gate.shape[3]
    hot = placement.shape[0]
    room = slot_room(count, expert_ids.shape[1], experts)
    half = -(-room // 2)
    room_a, room_b = round_up(room, 16), round_up(half, 16)
    per = room_a + room_b
    flip = me if experts <= DIRECT_LIMIT else jnp.int32(0)
    here = jnp.stack([flip, me, lax.axis_index("dp").astype(I32)])

    sds = jax.ShapeDtypeStruct
    scalars, high, low, *pieces = pl.pallas_call(
        functools.partial(route_kernel, (experts, hot, room, half, room_a, room_b)),
        out_shape=[sds((2,), I32)]
        + [sds((count, experts * per), BF16)] * 2
        + [sds((per, cols), BF16)] * experts,
        in_specs=[SMEM_SPEC] * 3 + vmem_specs(4),
        out_specs=[SMEM_SPEC] + vmem_specs(2 + experts),
        compiler_params=PARAMS,
        name="route",
    )(here, placement.T, capacity, expert_ids.T, replica_choice.T, gate_weights.T, tokens)
    arrived = exchange(pieces, "expert")

    rows_a, rows = experts * room_a, experts * per
    block = ff // parts
    order = list(range(parts - 1, 0, -1)) + [0]
    staged = pl.pallas_call(
        stage_kernel,
        out_shape=[sds((2, cols, 2 * block), BF16)] * parts,
        in_specs=[SMEM_SPEC] + [pl.BlockSpec(memory_space=pl.ANY)] * 2,
        out_specs=vmem_specs(parts),
        scratch_shapes=[pltpu.SemaphoreType.DMA((4 * parts,))],
        compiler_params=PARAMS,
        cost_estimate=cost(0, 16 * cols * ff),
        name="stage",
    )(scalars, w_gate, w_up)

    step = 2 * rows * cols * block
    sums = {}
    for i, k in enumerate(order):
        piece = sds((rows, 2 * block), BF16 if k else F32)
        halves = [sds((rows_a, cols), BF16), sds((rows - rows_a, cols), BF16)]
        made = pl.pallas_call(
            up_next_kernel
            if i
            else functools.partial(up_first_kernel, (experts, room_a, room_b)),
            out_shape=[piece] + ([] if i else halves),
            in_specs=vmem_specs(3 if i else experts + 1),
            out_specs=vmem_specs(1 if i else 3),
            compiler_params=PARAMS,
            cost_estimate=cost(2 * step, rows * (cols + 2 * block) * 2),
            name="up",
        )(*([xa, xb] if i else arrived), staged[k])
        sums[k] = made[0]
        if not i:
            xa, xb = made[1:]
        if k:
            sums[k] = lax.ppermute(sums[k], "dp", flips(parts, k))
    hidden = pl.pallas_call(
        hidden_kernel,
        out_shape=sds((rows, block), BF16),
        in_specs=vmem_specs(parts),
        out_specs=vmem_specs(1)[0],
        compiler_params=PARAMS,
        name="hidden",
    )(*[sums[k] for k in range(parts)])
    spread = {0: hidden}
    for k in order[:-1]:
        spread[k] = lax.ppermute(hidden, "dp", flips(parts, k))

    def down(kernel, k_list, operands, out_shape):
        specs = [pl.BlockSpec(x.shape, lambda f, s: (0, 0)) for x in operands]
        for k in k_list:
            for i in range(2):
                pick = lambda f, s, k=k, i=i: (0, s[1] * i, s[0] ^ k, 0)
                specs.append(pl.BlockSpec((1, 1, block, cols), pick))
        return pl.pallas_call(
            kernel,
            out_shape=out_shape,
            grid_spec=pltpu.PrefetchScalarGridSpec(
                num_scalar_prefetch=1,
                grid=(1,),
                in_specs=specs,
                out_specs=[pl.BlockSpec(x.shape, lambda f, s: (0, 0)) for x in out_shape],
            ),
            compiler_params=PARAMS,
            cost_estimate=cost(len(k_list) * step, rows * cols * 4),
            name="down",
        )(scalars, *operands, *([w_down] * (2 * len(k_list))))

    early, late = list(range(parts - 1)), [parts - 1]
    (acc,) = down(
        functools.partial(down_first_kernel, len(early), rows_a),
        early,
        [spread[k] for k in early],
        [sds((rows, cols), F32)],
    )
    results = down(
        functools.partial(down_last_kernel, len(late), (experts, room_a, room_b)),
        late,
        [acc] + [spread[k] for k in late],
        [sds((per, cols), BF16)] * experts,
    )
    returned = exchange(results, "expert")
    return pl.pallas_call(
        combine_kernel,
        out_shape=sds((count, cols), BF16),
        in_specs=vmem_specs(2 + experts),
        out_specs=vmem_specs(1)[0],
        scratch_shapes=[pltpu.VMEM((experts * per, cols), BF16)],
        compiler_params=PARAMS,
        name="combine",
    )(high, low, *returned)


def solution(mesh):
    return jax.shard_map(
        on_device,
        mesh=mesh,
        in_specs=(
            P("expert", "dp"),
            P("expert", None),
            P("expert", None),
            P("expert", None),
            P(),
            P(),
            P("expert", None, "dp", None),
            P("expert", None, "dp", None),
            P("expert", None, None, "dp"),
        ),
        out_specs=P("expert", "dp"),
        check_vma=False,
    )
```

```python
import functools

import jax
import jax.numpy as jnp
from jax import lax
from jax.experimental import pallas as pl
from jax.experimental.pallas import tpu as pltpu
from jax.sharding import PartitionSpec as P


BF16 = jnp.bfloat16
F32 = jnp.float32
I32 = jnp.int32
DIRECT_LIMIT = 8


def round_up(n, m):
    return -(-n // m) * m


def slot_room(token_count, top_count, expert_count):
    return max(2, min(token_count // 4, 3 * token_count * top_count // (4 * expert_count)))


def dot(a, b):
    return jnp.dot(a, b, preferred_element_type=F32)


def vmem_specs(n):
    return [pl.BlockSpec(memory_space=pltpu.VMEM)] * n


PARAMS = pltpu.CompilerParams(vmem_limit_bytes=24 * 2**20)


def in_hbm(x):
    return pltpu.with_memory_space_constraint(x, pltpu.HBM)


def cost(flops, size):
    return pl.CostEstimate(flops=flops, bytes_accessed=size, transcendentals=0)


SMEM_SPEC = pl.BlockSpec(memory_space=pltpu.SMEM)


def route_kernel(
    sizes, chunks, place_in, cap_in, ids_in, choice_in, gate_in, tok_in, second, *refs
):
    experts, hot, _, half, room_a, room_b, direct = sizes
    n = len(chunks)
    mats, pieces = refs[: 2 * n], refs[2 * n : 2 * n + experts]
    place, cap, ids_ref, choice_ref, gate_ref, tok_ref, sems = refs[2 * n + experts :]
    copies = [
        pltpu.make_async_copy(src, dst, sems.at[i])
        for i, (src, dst) in enumerate(
            (
                (ids_in, ids_ref),
                (choice_in, choice_ref),
                (gate_in, gate_ref),
                (place_in, place),
                (cap_in, cap),
                (tok_in, tok_ref),
            )
        )
    ]
    for copy in copies:
        copy.start()
    top, count = ids_ref.shape
    per = room_a + room_b
    me = lax.axis_index("expert")
    earlier = lax.broadcasted_iota(I32, (count, count), 1) < lax.broadcasted_iota(
        I32, (count, count), 0
    )
    lane = lax.broadcasted_iota(I32, (count, 2 * experts), 1).astype(F32)
    lane_row = lax.broadcasted_iota(I32, (1, 2 * experts), 1)
    for copy in copies[:5]:
        copy.wait()
    hosting = jnp.int32(0)
    for j in range(hot):
        hosting = jnp.where(place[1, j] == me, 1, hosting)
    second[0] = lax.axis_index("dp")
    second[1] = hosting
    key = (ids_ref[...] + experts * choice_ref[...]).astype(F32).T
    gate = gate_ref[...].T
    member = jnp.zeros((count, 2 * experts), F32)
    weight = jnp.zeros((count, 2 * experts), F32)
    for k in range(top):
        hit = key[:, k : k + 1] == lane
        member = jnp.where(hit, 1.0, member)
        weight = jnp.where(hit, gate[:, k : k + 1], weight)
    rank = dot(jnp.where(earlier, 1.0, 0.0).astype(BF16), member.astype(BF16))
    limit = jnp.zeros((1, 2 * experts), I32)
    for e in range(experts):
        limit = jnp.where(lane_row == e, cap[e], limit)
    for j in range(hot):
        limit = jnp.where(lane_row == place[0, j] + experts, cap[experts + j], limit)
    kept = (member > 0.5) & (rank < limit.astype(F32))
    rank = jnp.where(kept, rank, -1.0).astype(BF16)
    weight_high = weight.astype(BF16)
    weight_low = (weight - weight_high.astype(F32)).astype(BF16)

    done = 0
    for c, chunk in enumerate(chunks):
        columns = len(chunk) * per
        column = lax.broadcasted_iota(I32, (1, columns), 1)
        block = jnp.floor((column.astype(F32) + 0.5) * (1.0 / per)).astype(I32)
        slot = column - block * per
        if direct:
            flip = jnp.zeros((1, columns), I32)
            for i, j in enumerate(chunk):
                flip = jnp.where(block == i, j, flip)
            dest = flip ^ me
        else:
            dest = block + chunk[0]
        pair_key = jnp.full((1, columns), -1, I32)
        start = jnp.zeros((1, columns), I32)
        for j in range(hot):
            owner, host = dest == place[0, j], dest == place[1, j]
            pair_key = jnp.where(owner | host, place[0, j] + experts, pair_key)
            start = jnp.where(host, half, start)
        first = slot < room_a
        in_pair = slot - room_a
        wanted = jnp.where(first, dest, jnp.where(in_pair < half, pair_key, -1))
        place_rank = jnp.where(first, slot, in_pair + start).astype(F32)
        spread = jnp.where(
            lax.broadcasted_iota(I32, (2 * experts, columns), 0) == wanted, 1.0, 0.0
        ).astype(BF16)
        chosen = (dot(rank, spread) == place_rank) & (wanted >= 0)
        mats[2 * c][...] = jnp.where(chosen, dot(weight_high, spread), 0.0).astype(BF16)
        mats[2 * c + 1][...] = jnp.where(chosen, dot(weight_low, spread), 0.0).astype(BF16)
        picks = jnp.where(chosen, 1.0, 0.0).T.astype(BF16)
        if not c:
            copies[5].wait()
        rows = dot(picks, tok_ref[...]).astype(BF16)
        for i in range(len(chunk)):
            pieces[done + i][...] = rows[i * per : (i + 1) * per]
        done += len(chunk)


def stage_kernel(at, w_gate, w_up, *refs):
    outs, sems = refs[:-1], refs[-1]
    block = outs[0].shape[2] // 2
    copies = []
    for k, out in enumerate(outs):
        columns = pl.ds(pl.multiple_of((at[0] ^ k) * block, block), block)
        for i, which in enumerate((0, at[1])):
            for g, w in enumerate((w_gate, w_up)):
                copies.append(
                    pltpu.make_async_copy(
                        w.at[0, which, :, columns],
                        out.at[i, :, pl.ds(g * block, block)],
                        sems.at[len(copies)],
                    )
                )
    for copy in copies:
        copy.start()
    for copy in copies:
        copy.wait()


def up_sums(xa, xb, weights, out):
    rows_a = xa.shape[0]
    out[:rows_a] = dot(xa, weights[0]).astype(out.dtype)
    out[rows_a:] = dot(xb, weights[1]).astype(out.dtype)


def up_first_kernel(sizes, *refs):
    blocks, room_a, room_b = sizes
    x_refs, weights = refs[:blocks], refs[blocks]
    out, xa, xb = refs[blocks + 1 :]
    for i, ref in enumerate(x_refs):
        xa[i * room_a : (i + 1) * room_a] = ref[:room_a]
        xb[i * room_b : (i + 1) * room_b] = ref[room_a:]
    up_sums(xa[...], xb[...], weights, out)


def up_next_kernel(xa, xb, weights, out):
    up_sums(xa[...], xb[...], weights, out)


def hidden_kernel(own, *refs):
    out = refs[-1]
    block = own.shape[1] // 2
    total = own[...]
    for ref in refs[:-1]:
        total += ref[...].astype(F32)
    out[...] = (jax.nn.silu(total[:, :block]) * total[:, block:]).astype(BF16)


def down_kernel(sizes, at, w, *refs):
    parts, blocks, room_a, room_b = sizes
    hids, outs = refs[:parts], refs[parts:]
    rows_a, depth = blocks * room_a, hids[0].shape[1]
    ra = rb = 0.0
    for k, h in enumerate(hids):
        units = pl.ds(pl.multiple_of((at[0] ^ k) * depth, depth), depth)
        ra += dot(h[:rows_a], w[0, 0, units])
        rb += dot(h[rows_a:], w[0, at[1], units])
    ra, rb = ra.astype(BF16), rb.astype(BF16)
    for i, out in enumerate(outs):
        out[:room_a] = ra[i * room_a : (i + 1) * room_a]
        out[room_a:] = rb[i * room_b : (i + 1) * room_b]


def combine_kernel(has_base, *refs):
    base, (high, low) = refs[:has_base], refs[has_base : has_base + 2]
    pieces, out, res = refs[has_base + 2 : -2], refs[-2], refs[-1]
    per = pieces[0].shape[0]
    for i, ref in enumerate(pieces):
        res[i * per : (i + 1) * per] = ref[...]
    rows = res[...]
    total = dot(high[...], rows) + dot(low[...], rows)
    for ref in base:
        total += ref[...]
    out[...] = total.astype(out.dtype)


def flips(n, j):
    return [(i, i ^ j) for i in range(n)]


def exchange(pieces, chunks, axis):
    n = len(pieces)
    if n > DIRECT_LIMIT:
        moved = lax.all_to_all(jnp.stack(pieces), axis, split_axis=0, concat_axis=0, tiled=True)
        return [moved[i] for i in range(n)]
    moved = []
    for j, piece in zip([j for chunk in chunks for j in chunk], pieces):
        moved.append(lax.ppermute(piece, axis, flips(n, j)) if j else piece)
    return moved


def chunks_of(experts):
    if experts == 8:
        return ((4, 5, 1, 0), (2, 3, 6, 7))
    return (tuple(range(experts)),)


def on_device(
    tokens, expert_ids, replica_choice, gate_weights, placement, capacity, w_gate, w_up, w_down
):
    experts = lax.axis_size("expert")
    parts = lax.axis_size("dp")
    count, cols = tokens.shape
    ff = w_gate.shape[3]
    hot = placement.shape[0]
    room = slot_room(count, expert_ids.shape[1], experts)
    half = -(-room // 2)
    room_a, room_b = round_up(room, 16), round_up(half, 16)
    per = room_a + room_b
    chunks = chunks_of(experts)
    sds = jax.ShapeDtypeStruct
    hbm = pl.BlockSpec(memory_space=pltpu.HBM)
    top = expert_ids.shape[1]
    mat_shapes = [sds((count, len(c) * per), BF16) for c in chunks for _ in range(2)]
    scalars, *made = pl.pallas_call(
        functools.partial(
            route_kernel,
            (experts, hot, room, half, room_a, room_b, experts <= DIRECT_LIMIT),
            chunks,
        ),
        out_shape=[sds((2,), I32)] + mat_shapes + [sds((per, cols), BF16)] * experts,
        in_specs=[hbm] * 6,
        out_specs=[SMEM_SPEC] + vmem_specs(len(mat_shapes) + experts),
        scratch_shapes=[
            pltpu.SMEM((2, hot), I32),
            pltpu.SMEM(capacity.shape, I32),
            pltpu.VMEM((top, count), I32),
            pltpu.VMEM((top, count), I32),
            pltpu.VMEM((top, count), F32),
            pltpu.VMEM((count, cols), BF16),
            pltpu.SemaphoreType.DMA((6,)),
        ],
        compiler_params=PARAMS,
        name="route",
    )(
        *map(
            in_hbm,
            (placement.T, capacity, expert_ids.T, replica_choice.T, gate_weights.T, tokens),
        )
    )
    mats, pieces = made[: len(mat_shapes)], made[len(mat_shapes) :]
    arrived = exchange(pieces, chunks, "expert")

    block = ff // parts
    order = list(range(parts - 1, 0, -1)) + [0]
    staged = pl.pallas_call(
        stage_kernel,
        out_shape=[sds((2, cols, 2 * block), BF16)] * parts,
        in_specs=[SMEM_SPEC] + [hbm] * 2,
        out_specs=vmem_specs(parts),
        scratch_shapes=[pltpu.SemaphoreType.DMA((4 * parts,))],
        compiler_params=PARAMS,
        cost_estimate=cost(0, 16 * cols * ff),
        name="stage",
    )(scalars, in_hbm(w_gate), in_hbm(w_up))

    results, done = [], 0
    for chunk in chunks:
        blocks = len(chunk)
        rows_a, rows = blocks * room_a, blocks * per
        step = 2 * rows * cols * block
        sums = {}
        for i, k in enumerate(order):
            piece = sds((rows, 2 * block), BF16 if k else F32)
            halves = [sds((rows_a, cols), BF16), sds((rows - rows_a, cols), BF16)]
            made = pl.pallas_call(
                up_next_kernel
                if i
                else functools.partial(up_first_kernel, (blocks, room_a, room_b)),
                out_shape=[piece] + ([] if i else halves),
                in_specs=vmem_specs(3 if i else blocks + 1),
                out_specs=vmem_specs(1 if i else 3),
                compiler_params=PARAMS,
                cost_estimate=cost(2 * step, rows * (cols + 2 * block) * 2),
                name="up",
            )(*([xa, xb] if i else arrived[done : done + blocks]), staged[k])
            sums[k] = made[0]
            if not i:
                xa, xb = made[1:]
            if k:
                sums[k] = lax.ppermute(sums[k], "dp", flips(parts, k))
        hidden = pl.pallas_call(
            hidden_kernel,
            out_shape=sds((rows, block), BF16),
            in_specs=vmem_specs(parts),
            out_specs=vmem_specs(1)[0],
            compiler_params=PARAMS,
            name="hidden",
        )(*[sums[k] for k in range(parts)])
        spread = {0: hidden}
        for k in order[:-1]:
            spread[k] = lax.ppermute(hidden, "dp", flips(parts, k))
        results += pl.pallas_call(
            functools.partial(down_kernel, (parts, blocks, room_a, room_b)),
            out_shape=[sds((per, cols), BF16)] * blocks,
            in_specs=[SMEM_SPEC] + vmem_specs(1 + parts),
            out_specs=vmem_specs(blocks),
            compiler_params=PARAMS,
            cost_estimate=cost(parts * step, 4 * cols * ff),
            name="down",
        )(scalars, w_down, *[spread[k] for k in range(parts)])
        done += blocks
    returned = exchange(results, chunks, "expert")
    total, done = [], 0
    for c, chunk in enumerate(chunks):
        last = c + 1 == len(chunks)
        total = [
            pl.pallas_call(
                functools.partial(combine_kernel, len(total)),
                out_shape=sds((count, cols), BF16 if last else F32),
                in_specs=vmem_specs(len(total) + 2 + len(chunk)),
                out_specs=vmem_specs(1)[0],
                scratch_shapes=[pltpu.VMEM((len(chunk) * per, cols), BF16)],
                compiler_params=PARAMS,
                name="combine",
            )(*total, *mats[2 * c : 2 * c + 2], *returned[done : done + len(chunk)])
        ]
        done += len(chunk)
    return total[0]


def solution(mesh):
    return jax.shard_map(
        on_device,
        mesh=mesh,
        in_specs=(
            P("expert", "dp"),
            P("expert", None),
            P("expert", None),
            P("expert", None),
            P(),
            P(),
            P("expert", None, "dp", None),
            P("expert", None, "dp", None),
            P("expert", None, None, "dp"),
        ),
        out_specs=P("expert", "dp"),
        check_vma=False,
    )
```

```python
import functools

import jax
import jax.numpy as jnp
from jax import lax
from jax.experimental import pallas as pl
from jax.experimental.pallas import tpu as pltpu
from jax.sharding import PartitionSpec as P


BF16 = jnp.bfloat16
F32 = jnp.float32
I32 = jnp.int32
DIRECT_LIMIT = 8


def round_up(n, m):
    return -(-n // m) * m


def slot_room(token_count, top_count, expert_count):
    return max(2, min(token_count // 4, 3 * token_count * top_count // (4 * expert_count)))


def dot(a, b):
    return jnp.dot(a, b, preferred_element_type=F32)


def vmem_specs(n):
    return [pl.BlockSpec(memory_space=pltpu.VMEM)] * n


PARAMS = pltpu.CompilerParams(vmem_limit_bytes=24 * 2**20)


def in_hbm(x):
    return pltpu.with_memory_space_constraint(x, pltpu.HBM)


def cost(flops, size):
    return pl.CostEstimate(flops=flops, bytes_accessed=size, transcendentals=0)


def slots_of(sizes, place, cap, ids_ref, choice_ref):
    experts, hot = sizes[:2]
    top, count = ids_ref.shape
    key = (ids_ref[...] + experts * choice_ref[...]).astype(F32).T
    lane = lax.broadcasted_iota(I32, (count, 2 * experts), 1).astype(F32)
    hits = [key[:, k : k + 1] == lane for k in range(top)]
    member = jnp.zeros((count, 2 * experts), F32)
    for hit in hits:
        member = jnp.where(hit, 1.0, member)
    earlier = lax.broadcasted_iota(I32, (count, count), 1) < lax.broadcasted_iota(
        I32, (count, count), 0
    )
    rank = dot(jnp.where(earlier, 1.0, 0.0).astype(BF16), member.astype(BF16))
    lane_row = lax.broadcasted_iota(I32, (1, 2 * experts), 1)
    limit = jnp.zeros((1, 2 * experts), I32)
    for e in range(experts):
        limit = jnp.where(lane_row == e, cap[e], limit)
    for j in range(hot):
        limit = jnp.where(lane_row == place[0, j] + experts, cap[experts + j], limit)
    kept = (member > 0.5) & (rank < limit.astype(F32))
    return jnp.where(kept, rank, -1.0).astype(BF16), hits


def columns_of(sizes, place, chunk):
    experts, hot, _, half, room_a, room_b, direct = sizes
    per = room_a + room_b
    columns = len(chunk) * per
    column = lax.broadcasted_iota(I32, (1, columns), 1)
    block = jnp.floor((column.astype(F32) + 0.5) * (1.0 / per)).astype(I32)
    slot = column - block * per
    if direct:
        flip = jnp.zeros((1, columns), I32)
        for i, j in enumerate(chunk):
            flip = jnp.where(block == i, j, flip)
        dest = flip ^ lax.axis_index("expert")
    else:
        dest = block + chunk[0]
    pair_key = jnp.full((1, columns), -1, I32)
    start = jnp.zeros((1, columns), I32)
    for j in range(hot):
        owner, host = dest == place[0, j], dest == place[1, j]
        pair_key = jnp.where(owner | host, place[0, j] + experts, pair_key)
        start = jnp.where(host, half, start)
    first = slot < room_a
    in_pair = slot - room_a
    wanted = jnp.where(first, dest, jnp.where(in_pair < half, pair_key, -1))
    place_rank = jnp.where(first, slot, in_pair + start).astype(F32)
    place_rank = jnp.where(wanted >= 0, place_rank, -2.0)
    spread = jnp.where(
        lax.broadcasted_iota(I32, (2 * experts, columns), 0) == wanted, 1.0, 0.0
    ).astype(BF16)
    return spread, place_rank


def fetch(pairs, sems):
    copies = [
        pltpu.make_async_copy(src, dst, sems.at[i]) for i, (src, dst) in enumerate(pairs)
    ]
    for copy in copies:
        copy.start()
    return copies


def route_kernel(sizes, chunks, place_in, cap_in, ids_in, choice_in, tok_in, *refs):
    pieces = refs[:-6]
    place, cap, ids_ref, choice_ref, tok_ref, sems = refs[-6:]
    copies = fetch(
        (
            (ids_in, ids_ref),
            (choice_in, choice_ref),
            (place_in, place),
            (cap_in, cap),
            (tok_in, tok_ref),
        ),
        sems,
    )
    for copy in copies[:4]:
        copy.wait()
    rank, _ = slots_of(sizes, place, cap, ids_ref, choice_ref)
    per = pieces[0].shape[0]
    done = 0
    for chunk in chunks:
        spread, place_rank = columns_of(sizes, place, chunk)
        picks = jnp.where(dot(rank, spread) == place_rank, 1.0, 0.0).T.astype(BF16)
        if not done:
            copies[4].wait()
        rows = dot(picks, tok_ref[...]).astype(BF16)
        for i in range(len(chunk)):
            pieces[done + i][...] = rows[i * per : (i + 1) * per]
        done += len(chunk)


def weigh_kernel(sizes, chunks, place_in, cap_in, ids_in, choice_in, gate_in, *refs):
    mats = refs[:-6]
    place, cap, ids_ref, choice_ref, gate_ref, sems = refs[-6:]
    copies = fetch(
        (
            (ids_in, ids_ref),
            (choice_in, choice_ref),
            (place_in, place),
            (cap_in, cap),
            (gate_in, gate_ref),
        ),
        sems,
    )
    for copy in copies:
        copy.wait()
    rank, hits = slots_of(sizes, place, cap, ids_ref, choice_ref)
    gate = gate_ref[...].T
    weight = jnp.zeros(rank.shape, F32)
    for k, hit in enumerate(hits):
        weight = jnp.where(hit, gate[:, k : k + 1], weight)
    weight_high = weight.astype(BF16)
    weight_low = (weight - weight_high.astype(F32)).astype(BF16)
    for c, chunk in enumerate(chunks):
        spread, place_rank = columns_of(sizes, place, chunk)
        chosen = dot(rank, spread) == place_rank
        for part, out in zip((weight_high, weight_low), mats[2 * c : 2 * c + 2]):
            out[...] = jnp.where(chosen, dot(part, spread), 0.0).astype(BF16)


def hosting(place):
    found = jnp.int32(0)
    for j in range(place.shape[1]):
        found = jnp.where(place[1, j] == lax.axis_index("expert"), 1, found)
    return found


def stage_weights(place_in, place, sems, moves):
    looked = pltpu.make_async_copy(place_in, place, sems.at[0])
    looked.start()
    copies = []

    def begin(which, i):
        for src, dst in moves(which, i):
            copies.append(pltpu.make_async_copy(src, dst, sems.at[len(copies) + 1]))
            copies[-1].start()

    begin(0, 0)
    looked.wait()
    begin(hosting(place), 1)
    for copy in copies:
        copy.wait()


def stage_kernel(place_in, w_gate, w_up, *refs):
    outs, place, sems = refs[:-2], refs[-2], refs[-1]
    block = outs[0].shape[2] // 2

    def moves(which, i):
        for k, out in enumerate(outs):
            q = lax.axis_index("dp") ^ k
            columns = pl.ds(pl.multiple_of(q * block, block), block)
            for g, w in enumerate((w_gate, w_up)):
                yield w.at[0, which, :, columns], out.at[i, :, pl.ds(g * block, block)]

    stage_weights(place_in, place, sems, moves)


def stage_down_kernel(parts, place_in, w_down, out, place, sems):
    block = out.shape[1] // parts

    def moves(which, i):
        for k in range(parts):
            q = lax.axis_index("dp") ^ k
            units = pl.ds(pl.multiple_of(q * block, block), block)
            yield w_down.at[0, which, units], out.at[i, pl.ds(k * block, block)]

    stage_weights(place_in, place, sems, moves)


def up_sums(xa, xb, weights, out):
    rows_a = xa.shape[0]
    out[:rows_a] = dot(xa, weights[0]).astype(out.dtype)
    out[rows_a:] = dot(xb, weights[1]).astype(out.dtype)


def up_first_kernel(sizes, *refs):
    blocks, room_a, room_b = sizes
    x_refs, weights = refs[:blocks], refs[blocks]
    out, xa, xb = refs[blocks + 1 :]
    for i, ref in enumerate(x_refs):
        xa[i * room_a : (i + 1) * room_a] = ref[:room_a]
        xb[i * room_b : (i + 1) * room_b] = ref[room_a:]
    up_sums(xa[...], xb[...], weights, out)


def up_next_kernel(xa, xb, weights, out):
    up_sums(xa[...], xb[...], weights, out)


def hidden_kernel(own, *refs):
    out = refs[-1]
    block = own.shape[1] // 2
    total = own[...]
    for ref in refs[:-1]:
        total += ref[...].astype(F32)
    out[...] = (jax.nn.silu(total[:, :block]) * total[:, block:]).astype(BF16)


def down_kernel(sizes, w, *refs):
    parts, blocks, room_a, room_b = sizes
    hids, outs, full = refs[:parts], refs[parts:-1], refs[-1]
    rows_a, depth = blocks * room_a, hids[0].shape[1]
    for k, h in enumerate(hids):
        full[:, k * depth : (k + 1) * depth] = h[...]
    ra = dot(full[:rows_a], w[0]).astype(BF16)
    rb = dot(full[rows_a:], w[1]).astype(BF16)
    for i, out in enumerate(outs):
        out[:room_a] = ra[i * room_a : (i + 1) * room_a]
        out[room_a:] = rb[i * room_b : (i + 1) * room_b]


def combine_kernel(has_base, *refs):
    base, (high, low) = refs[:has_base], refs[has_base : has_base + 2]
    pieces, out, res = refs[has_base + 2 : -2], refs[-2], refs[-1]
    per = pieces[0].shape[0]
    for i, ref in enumerate(pieces):
        res[i * per : (i + 1) * per] = ref[...]
    rows = res[...]
    total = dot(high[...], rows) + dot(low[...], rows)
    for ref in base:
        total += ref[...]
    out[...] = total.astype(out.dtype)


def flips(n, j):
    return [(i, i ^ j) for i in range(n)]


def exchange(pieces, chunks, axis):
    n = len(pieces)
    if n > DIRECT_LIMIT:
        moved = lax.all_to_all(jnp.stack(pieces), axis, split_axis=0, concat_axis=0, tiled=True)
        return [moved[i] for i in range(n)]
    moved = []
    for j, piece in zip([j for chunk in chunks for j in chunk], pieces):
        moved.append(lax.ppermute(piece, axis, flips(n, j)) if j else piece)
    return moved


def chunks_of(experts):
    if experts == 8:
        return ((4, 5, 1, 0), (2, 3, 6, 7))
    return (tuple(range(experts)),)


def on_device(
    tokens, expert_ids, replica_choice, gate_weights, placement, capacity, w_gate, w_up, w_down
):
    experts = lax.axis_size("expert")
    parts = lax.axis_size("dp")
    count, cols = tokens.shape
    ff = w_gate.shape[3]
    hot = placement.shape[0]
    room = slot_room(count, expert_ids.shape[1], experts)
    half = -(-room // 2)
    room_a, room_b = round_up(room, 16), round_up(half, 16)
    per = room_a + room_b
    chunks = chunks_of(experts)
    sds = jax.ShapeDtypeStruct
    hbm = pl.BlockSpec(memory_space=pltpu.HBM)
    top = expert_ids.shape[1]
    sizes = (experts, hot, room, half, room_a, room_b, experts <= DIRECT_LIMIT)
    small = [placement.T, capacity, expert_ids.T, replica_choice.T]
    small_scratch = [
        pltpu.SMEM((2, hot), I32),
        pltpu.SMEM(capacity.shape, I32),
        pltpu.VMEM((top, count), I32),
        pltpu.VMEM((top, count), I32),
    ]
    pieces = pl.pallas_call(
        functools.partial(route_kernel, sizes, chunks),
        out_shape=[sds((per, cols), BF16)] * experts,
        in_specs=[hbm] * 5,
        out_specs=vmem_specs(experts),
        scratch_shapes=small_scratch
        + [pltpu.VMEM((count, cols), BF16), pltpu.SemaphoreType.DMA((5,))],
        compiler_params=PARAMS,
        name="route",
    )(*map(in_hbm, [*small, tokens]))
    mat_shapes = [sds((count, len(c) * per), BF16) for c in chunks for _ in range(2)]
    mats = pl.pallas_call(
        functools.partial(weigh_kernel, sizes, chunks),
        out_shape=mat_shapes,
        in_specs=[hbm] * 5,
        out_specs=vmem_specs(len(mat_shapes)),
        scratch_shapes=small_scratch
        + [pltpu.VMEM((top, count), F32), pltpu.SemaphoreType.DMA((5,))],
        compiler_params=PARAMS,
        name="weigh",
    )(*map(in_hbm, [*small, gate_weights.T]))
    arrived = exchange(pieces, chunks, "expert")

    block = ff // parts
    order = list(range(parts - 1, 0, -1)) + [0]
    staged = pl.pallas_call(
        stage_kernel,
        out_shape=[sds((2, cols, 2 * block), BF16)] * parts,
        in_specs=[hbm] * 3,
        out_specs=vmem_specs(parts),
        scratch_shapes=[pltpu.SMEM((2, hot), I32), pltpu.SemaphoreType.DMA((4 * parts + 1,))],
        compiler_params=PARAMS,
        cost_estimate=cost(0, 16 * cols * ff),
        name="stage",
    )(*map(in_hbm, [placement.T, w_gate, w_up]))
    staged_down = pl.pallas_call(
        functools.partial(stage_down_kernel, parts),
        out_shape=sds((2, ff, cols), BF16),
        in_specs=[hbm] * 2,
        out_specs=vmem_specs(1)[0],
        scratch_shapes=[pltpu.SMEM((2, hot), I32), pltpu.SemaphoreType.DMA((2 * parts + 1,))],
        compiler_params=PARAMS,
        cost_estimate=cost(0, 8 * cols * ff),
        name="stage_down",
    )(*map(in_hbm, [placement.T, w_down]))

    results, done = [], 0
    for chunk in chunks:
        blocks = len(chunk)
        rows_a, rows = blocks * room_a, blocks * per
        step = 2 * rows * cols * block
        sums = {}
        for i, k in enumerate(order):
            piece = sds((rows, 2 * block), BF16 if k else F32)
            halves = [sds((rows_a, cols), BF16), sds((rows - rows_a, cols), BF16)]
            made = pl.pallas_call(
                up_next_kernel
                if i
                else functools.partial(up_first_kernel, (blocks, room_a, room_b)),
                out_shape=[piece] + ([] if i else halves),
                in_specs=vmem_specs(3 if i else blocks + 1),
                out_specs=vmem_specs(1 if i else 3),
                compiler_params=PARAMS,
                cost_estimate=cost(2 * step, rows * (cols + 2 * block) * 2),
                name="up",
            )(*([xa, xb] if i else arrived[done : done + blocks]), staged[k])
            sums[k] = made[0]
            if not i:
                xa, xb = made[1:]
            if k:
                sums[k] = lax.ppermute(sums[k], "dp", flips(parts, k))
        hidden = pl.pallas_call(
            hidden_kernel,
            out_shape=sds((rows, block), BF16),
            in_specs=vmem_specs(parts),
            out_specs=vmem_specs(1)[0],
            compiler_params=PARAMS,
            name="hidden",
        )(*[sums[k] for k in range(parts)])
        spread = {0: hidden}
        for k in order[:-1]:
            spread[k] = lax.ppermute(hidden, "dp", flips(parts, k))
        results += pl.pallas_call(
            functools.partial(down_kernel, (parts, blocks, room_a, room_b)),
            out_shape=[sds((per, cols), BF16)] * blocks,
            in_specs=vmem_specs(1 + parts),
            out_specs=vmem_specs(blocks),
            scratch_shapes=[pltpu.VMEM((rows, ff), BF16)],
            compiler_params=PARAMS,
            cost_estimate=cost(parts * step, 4 * cols * ff),
            name="down",
        )(staged_down, *[spread[k] for k in range(parts)])
        done += blocks
    returned = exchange(results, chunks, "expert")
    total, done = [], 0
    for c, chunk in enumerate(chunks):
        last = c + 1 == len(chunks)
        total = [
            pl.pallas_call(
                functools.partial(combine_kernel, len(total)),
                out_shape=sds((count, cols), BF16 if last else F32),
                in_specs=vmem_specs(len(total) + 2 + len(chunk)),
                out_specs=vmem_specs(1)[0],
                scratch_shapes=[pltpu.VMEM((len(chunk) * per, cols), BF16)],
                compiler_params=PARAMS,
                name="combine",
            )(*total, *mats[2 * c : 2 * c + 2], *returned[done : done + len(chunk)])
        ]
        done += len(chunk)
    return total[0]


def solution(mesh):
    return jax.shard_map(
        on_device,
        mesh=mesh,
        in_specs=(
            P("expert", "dp"),
            P("expert", None),
            P("expert", None),
            P("expert", None),
            P(),
            P(),
            P("expert", None, "dp", None),
            P("expert", None, "dp", None),
            P("expert", None, None, "dp"),
        ),
        out_specs=P("expert", "dp"),
        check_vma=False,
    )
```

```python
import functools

import jax
import jax.numpy as jnp
from jax import lax
from jax.experimental import pallas as pl
from jax.experimental.pallas import tpu as pltpu
from jax.sharding import PartitionSpec as P


BF16 = jnp.bfloat16
F32 = jnp.float32
I32 = jnp.int32
DIRECT_LIMIT = 8


def round_up(n, m):
    return -(-n // m) * m


def slot_room(token_count, top_count, expert_count):
    return max(2, min(token_count // 4, 3 * token_count * top_count // (4 * expert_count)))


def dot(a, b):
    return jnp.dot(a, b, preferred_element_type=F32)


def vmem_specs(n):
    return [pl.BlockSpec(memory_space=pltpu.VMEM)] * n


PARAMS = pltpu.CompilerParams(vmem_limit_bytes=24 * 2**20)


def in_hbm(x):
    return pltpu.with_memory_space_constraint(x, pltpu.HBM)


def cost(flops, size):
    return pl.CostEstimate(flops=flops, bytes_accessed=size, transcendentals=0)


def slots_of(sizes, place, cap, ids_ref, choice_ref):
    experts, hot = sizes[:2]
    top, count = ids_ref.shape
    key = ids_ref[...] + experts * choice_ref[...]
    row = lax.broadcasted_iota(I32, (2 * experts, count), 0)
    hits = [key[k : k + 1] == row for k in range(top)]
    member = functools.reduce(jnp.logical_or, hits)
    later = lax.broadcasted_iota(I32, (count, count), 0) < lax.broadcasted_iota(
        I32, (count, count), 1
    )
    rank = dot(jnp.where(member, 1.0, 0.0).astype(BF16), jnp.where(later, 1.0, 0.0).astype(BF16))
    row_one = lax.broadcasted_iota(I32, (2 * experts, 1), 0)
    limit = jnp.zeros((2 * experts, 1), I32)
    for e in range(experts):
        limit = jnp.where(row_one == e, cap[e], limit)
    for j in range(hot):
        limit = jnp.where(row_one == place[0, j] + experts, cap[experts + j], limit)
    kept = member & (rank < limit.astype(F32))
    return jnp.where(kept, rank, -1.0), hits


def columns_of(sizes, place, chunk):
    experts, hot, _, half, room_a, room_b, direct = sizes
    per = room_a + room_b
    columns = len(chunk) * per
    column = lax.broadcasted_iota(I32, (1, columns), 1)
    block = jnp.floor((column.astype(F32) + 0.5) * (1.0 / per)).astype(I32)
    slot = column - block * per
    if direct:
        flip = jnp.zeros((1, columns), I32)
        for i, j in enumerate(chunk):
            flip = jnp.where(block == i, j, flip)
        dest = flip ^ lax.axis_index("expert")
    else:
        dest = block + chunk[0]
    pair_key = jnp.full((1, columns), -1, I32)
    start = jnp.zeros((1, columns), I32)
    for j in range(hot):
        owner, host = dest == place[0, j], dest == place[1, j]
        pair_key = jnp.where(owner | host, place[0, j] + experts, pair_key)
        start = jnp.where(host, half, start)
    first = slot < room_a
    in_pair = slot - room_a
    wanted = jnp.where(first, dest, jnp.where(in_pair < half, pair_key, -1))
    place_rank = jnp.where(first, slot, in_pair + start).astype(F32)
    place_rank = jnp.where(wanted >= 0, place_rank, -2.0)
    spread = jnp.where(
        lax.broadcasted_iota(I32, (2 * experts, columns), 0) == wanted, 1.0, 0.0
    )
    return spread, place_rank


def fetch(pairs, sems):
    copies = [
        pltpu.make_async_copy(src, dst, sems.at[i]) for i, (src, dst) in enumerate(pairs)
    ]
    for copy in copies:
        copy.start()
    return copies


def route_kernel(sizes, chunks, place_in, cap_in, ids_in, choice_in, tok_in, *refs):
    pieces = refs[:-6]
    place, cap, ids_ref, choice_ref, tok_ref, sems = refs[-6:]
    copies = fetch(
        (
            (ids_in, ids_ref),
            (choice_in, choice_ref),
            (place_in, place),
            (cap_in, cap),
            (tok_in, tok_ref),
        ),
        sems,
    )
    for copy in copies[:4]:
        copy.wait()
    spread, place_rank = columns_of(sizes, place, sum(chunks, ()))
    replicas = spread.shape[0]
    turned = jnp.concatenate([spread, jnp.broadcast_to(place_rank, (8, place_rank.shape[1]))]).T
    rank, _ = slots_of(sizes, place, cap, ids_ref, choice_ref)
    slot = dot(turned[:, :replicas].astype(BF16), rank.astype(BF16))
    picks = jnp.where(slot == turned[:, replicas : replicas + 1], 1.0, 0.0).astype(BF16)
    copies[4].wait()
    rows = dot(picks, tok_ref[...]).astype(BF16)
    per = pieces[0].shape[0]
    for i, piece in enumerate(pieces):
        piece[...] = rows[i * per : (i + 1) * per]


def weigh_kernel(sizes, chunks, place_in, cap_in, ids_in, choice_in, gate_in, *refs):
    mats = refs[:-6]
    place, cap, ids_ref, choice_ref, gate_ref, sems = refs[-6:]
    copies = fetch(
        (
            (ids_in, ids_ref),
            (choice_in, choice_ref),
            (place_in, place),
            (cap_in, cap),
            (gate_in, gate_ref),
        ),
        sems,
    )
    for copy in copies:
        copy.wait()
    rank, hits = slots_of(sizes, place, cap, ids_ref, choice_ref)
    weight = jnp.zeros(rank.shape, F32)
    for k, hit in enumerate(hits):
        weight = jnp.where(hit, gate_ref[k : k + 1], weight)
    weight, rank = weight.T, rank.T.astype(BF16)
    weight_high = weight.astype(BF16)
    weight_low = (weight - weight_high.astype(F32)).astype(BF16)
    for c, chunk in enumerate(chunks):
        spread, place_rank = columns_of(sizes, place, chunk)
        spread = spread.astype(BF16)
        chosen = dot(rank, spread) == place_rank
        for part, out in zip((weight_high, weight_low), mats[2 * c : 2 * c + 2]):
            out[...] = jnp.where(chosen, dot(part, spread), 0.0).astype(BF16)


def hosting(place):
    found = jnp.int32(0)
    for j in range(place.shape[1]):
        found = jnp.where(place[1, j] == lax.axis_index("expert"), 1, found)
    return found


def stage_weights(place_in, place, sems, moves):
    looked = pltpu.make_async_copy(place_in, place, sems.at[0])
    looked.start()
    copies = []

    def begin(which, i):
        for src, dst in moves(which, i):
            copies.append(pltpu.make_async_copy(src, dst, sems.at[len(copies) + 1]))
            copies[-1].start()

    begin(0, 0)
    looked.wait()
    begin(hosting(place), 1)
    for copy in copies:
        copy.wait()


def stage_kernel(place_in, w_gate, w_up, *refs):
    outs, place, sems = refs[:-2], refs[-2], refs[-1]
    block = outs[0].shape[2] // 2

    def moves(which, i):
        for k, out in enumerate(outs):
            q = lax.axis_index("dp") ^ role(k, len(outs), lax.axis_index("expert"))
            columns = pl.ds(pl.multiple_of(q * block, block), block)
            for g, w in enumerate((w_gate, w_up)):
                yield w.at[0, which, :, columns], out.at[i, :, pl.ds(g * block, block)]

    stage_weights(place_in, place, sems, moves)


def stage_down_kernel(parts, place_in, w_down, out, place, sems):
    block = out.shape[1] // parts

    def moves(which, i):
        for k in range(parts):
            q = lax.axis_index("dp") ^ role(k, parts, lax.axis_index("expert"))
            units = pl.ds(pl.multiple_of(q * block, block), block)
            yield w_down.at[0, which, units], out.at[i, pl.ds(k * block, block)]

    stage_weights(place_in, place, sems, moves)


def up_sums(xa, xb, weights, out):
    rows_a = xa.shape[0]
    out[:rows_a] = dot(xa, weights[0]).astype(out.dtype)
    out[rows_a:] = dot(xb, weights[1]).astype(out.dtype)


def up_first_kernel(sizes, *refs):
    blocks, room_a, room_b = sizes
    x_refs, weights = refs[:blocks], refs[blocks]
    out, xa, xb = refs[blocks + 1 :]
    for i, ref in enumerate(x_refs):
        xa[i * room_a : (i + 1) * room_a] = ref[:room_a]
        xb[i * room_b : (i + 1) * room_b] = ref[room_a:]
    up_sums(xa[...], xb[...], weights, out)


def up_next_kernel(xa, xb, weights, out):
    up_sums(xa[...], xb[...], weights, out)


def hidden_kernel(own, *refs):
    out = refs[-1]
    block = own.shape[1] // 2
    total = own[...]
    for ref in refs[:-1]:
        total += ref[...].astype(F32)
    out[...] = (jax.nn.silu(total[:, :block]) * total[:, block:]).astype(BF16)


def down_kernel(sizes, w, *refs):
    parts, blocks, room_a, room_b = sizes
    hids, outs, full = refs[:parts], refs[parts:-1], refs[-1]
    rows_a, depth = blocks * room_a, hids[0].shape[1]
    for k, h in enumerate(hids):
        full[:, k * depth : (k + 1) * depth] = h[...]
    ra = dot(full[:rows_a], w[0]).astype(BF16)
    rb = dot(full[rows_a:], w[1]).astype(BF16)
    for i, out in enumerate(outs):
        out[:room_a] = ra[i * room_a : (i + 1) * room_a]
        out[room_a:] = rb[i * room_b : (i + 1) * room_b]


def combine_kernel(has_base, *refs):
    base, (high, low) = refs[:has_base], refs[has_base : has_base + 2]
    pieces, out, res = refs[has_base + 2 : -2], refs[-2], refs[-1]
    per = pieces[0].shape[0]
    for i, ref in enumerate(pieces):
        res[i * per : (i + 1) * per] = ref[...]
    rows = res[...]
    total = dot(high[...], rows) + dot(low[...], rows)
    for ref in base:
        total += ref[...]
    out[...] = total.astype(out.dtype)


def flips(n, j):
    return [(i, i ^ j) for i in range(n)]


def role(k, parts, expert):
    if parts != 4 or k not in (1, 2):
        return k
    return k + (3 - 2 * k) * (expert % 2)


def to_partner(x, k):
    parts, experts = lax.axis_size("dp"), lax.axis_size("expert")
    pairs = [
        (p * experts + e, (p ^ role(k, parts, e)) * experts + e)
        for p in range(parts)
        for e in range(experts)
    ]
    return lax.ppermute(x, ("dp", "expert"), pairs)


def exchange(pieces, chunks, axis):
    n = len(pieces)
    if n > DIRECT_LIMIT:
        moved = lax.all_to_all(jnp.stack(pieces), axis, split_axis=0, concat_axis=0, tiled=True)
        return [moved[i] for i in range(n)]
    moved = []
    for j, piece in zip([j for chunk in chunks for j in chunk], pieces):
        moved.append(lax.ppermute(piece, axis, flips(n, j)) if j else piece)
    return moved


def chunks_of(experts):
    if experts == 8:
        return ((4, 5, 1, 0), (2, 3, 6, 7))
    return (tuple(range(experts)),)


def on_device(
    tokens, expert_ids, replica_choice, gate_weights, placement, capacity, w_gate, w_up, w_down
):
    experts = lax.axis_size("expert")
    parts = lax.axis_size("dp")
    count, cols = tokens.shape
    ff = w_gate.shape[3]
    hot = placement.shape[0]
    room = slot_room(count, expert_ids.shape[1], experts)
    half = -(-room // 2)
    room_a, room_b = round_up(room, 16), round_up(half, 16)
    per = room_a + room_b
    chunks = chunks_of(experts)
    sds = jax.ShapeDtypeStruct
    hbm = pl.BlockSpec(memory_space=pltpu.HBM)
    top = expert_ids.shape[1]
    sizes = (experts, hot, room, half, room_a, room_b, experts <= DIRECT_LIMIT)
    small = [placement.T, capacity, expert_ids.T, replica_choice.T]
    small_scratch = [
        pltpu.SMEM((2, hot), I32),
        pltpu.SMEM(capacity.shape, I32),
        pltpu.VMEM((top, count), I32),
        pltpu.VMEM((top, count), I32),
    ]
    pieces = pl.pallas_call(
        functools.partial(route_kernel, sizes, chunks),
        out_shape=[sds((per, cols), BF16)] * experts,
        in_specs=[hbm] * 5,
        out_specs=vmem_specs(experts),
        scratch_shapes=small_scratch
        + [pltpu.VMEM((count, cols), BF16), pltpu.SemaphoreType.DMA((5,))],
        compiler_params=PARAMS,
        name="route",
    )(*map(in_hbm, [*small, tokens]))
    mat_shapes = [sds((count, len(c) * per), BF16) for c in chunks for _ in range(2)]
    mats = pl.pallas_call(
        functools.partial(weigh_kernel, sizes, chunks),
        out_shape=mat_shapes,
        in_specs=[hbm] * 5,
        out_specs=vmem_specs(len(mat_shapes)),
        scratch_shapes=small_scratch
        + [pltpu.VMEM((top, count), F32), pltpu.SemaphoreType.DMA((5,))],
        compiler_params=PARAMS,
        name="weigh",
    )(*map(in_hbm, [*small, gate_weights.T]))
    arrived = exchange(pieces, chunks, "expert")

    block = ff // parts
    order = list(range(parts - 1, 0, -1)) + [0]
    staged = pl.pallas_call(
        stage_kernel,
        out_shape=[sds((2, cols, 2 * block), BF16)] * parts,
        in_specs=[hbm] * 3,
        out_specs=vmem_specs(parts),
        scratch_shapes=[pltpu.SMEM((2, hot), I32), pltpu.SemaphoreType.DMA((4 * parts + 1,))],
        compiler_params=PARAMS,
        cost_estimate=cost(0, 16 * cols * ff),
        name="stage",
    )(*map(in_hbm, [placement.T, w_gate, w_up]))
    staged_down = pl.pallas_call(
        functools.partial(stage_down_kernel, parts),
        out_shape=sds((2, ff, cols), BF16),
        in_specs=[hbm] * 2,
        out_specs=vmem_specs(1)[0],
        scratch_shapes=[pltpu.SMEM((2, hot), I32), pltpu.SemaphoreType.DMA((2 * parts + 1,))],
        compiler_params=PARAMS,
        cost_estimate=cost(0, 8 * cols * ff),
        name="stage_down",
    )(*map(in_hbm, [placement.T, w_down]))

    results, done = [], 0
    for chunk in chunks:
        blocks = len(chunk)
        rows_a, rows = blocks * room_a, blocks * per
        step = 2 * rows * cols * block
        sums = {}
        for i, k in enumerate(order):
            piece = sds((rows, 2 * block), BF16 if k else F32)
            halves = [sds((rows_a, cols), BF16), sds((rows - rows_a, cols), BF16)]
            made = pl.pallas_call(
                up_next_kernel
                if i
                else functools.partial(up_first_kernel, (blocks, room_a, room_b)),
                out_shape=[piece] + ([] if i else halves),
                in_specs=vmem_specs(3 if i else blocks + 1),
                out_specs=vmem_specs(1 if i else 3),
                compiler_params=PARAMS,
                cost_estimate=cost(2 * step, rows * (cols + 2 * block) * 2),
                name="up",
            )(*([xa, xb] if i else arrived[done : done + blocks]), staged[k])
            sums[k] = made[0]
            if not i:
                xa, xb = made[1:]
            if k:
                sums[k] = to_partner(sums[k], k)
        hidden = pl.pallas_call(
            hidden_kernel,
            out_shape=sds((rows, block), BF16),
            in_specs=vmem_specs(parts),
            out_specs=vmem_specs(1)[0],
            compiler_params=PARAMS,
            name="hidden",
        )(*[sums[k] for k in range(parts)])
        spread = {0: hidden}
        for k in order[:-1]:
            spread[k] = to_partner(hidden, k)
        results += pl.pallas_call(
            functools.partial(down_kernel, (parts, blocks, room_a, room_b)),
            out_shape=[sds((per, cols), BF16)] * blocks,
            in_specs=vmem_specs(1 + parts),
            out_specs=vmem_specs(blocks),
            scratch_shapes=[pltpu.VMEM((rows, ff), BF16)],
            compiler_params=PARAMS,
            cost_estimate=cost(parts * step, 4 * cols * ff),
            name="down",
        )(staged_down, *[spread[k] for k in range(parts)])
        done += blocks
    returned = exchange(results, chunks, "expert")
    total, done = [], 0
    for c, chunk in enumerate(chunks):
        last = c + 1 == len(chunks)
        total = [
            pl.pallas_call(
                functools.partial(combine_kernel, len(total)),
                out_shape=sds((count, cols), BF16 if last else F32),
                in_specs=vmem_specs(len(total) + 2 + len(chunk)),
                out_specs=vmem_specs(1)[0],
                scratch_shapes=[pltpu.VMEM((len(chunk) * per, cols), BF16)],
                compiler_params=PARAMS,
                name="combine",
            )(*total, *mats[2 * c : 2 * c + 2], *returned[done : done + len(chunk)])
        ]
        done += len(chunk)
    return total[0]


def solution(mesh):
    return jax.shard_map(
        on_device,
        mesh=mesh,
        in_specs=(
            P("expert", "dp"),
            P("expert", None),
            P("expert", None),
            P("expert", None),
            P(),
            P(),
            P("expert", None, "dp", None),
            P("expert", None, "dp", None),
            P("expert", None, None, "dp"),
        ),
        out_specs=P("expert", "dp"),
        check_vma=False,
    )
```

```python
import functools

import jax
import jax.numpy as jnp
from jax import lax
from jax.experimental import pallas as pl
from jax.experimental.pallas import tpu as pltpu
from jax.sharding import PartitionSpec as P


BF16 = jnp.bfloat16
F32 = jnp.float32
I32 = jnp.int32
DIRECT_LIMIT = 8


def round_up(n, m):
    return -(-n // m) * m


def slot_room(token_count, top_count, expert_count):
    return max(2, min(token_count // 4, 3 * token_count * top_count // (4 * expert_count)))


def dot(a, b):
    return jnp.dot(a, b, preferred_element_type=F32)


def vmem_specs(n):
    return [pl.BlockSpec(memory_space=pltpu.VMEM)] * n


PARAMS = pltpu.CompilerParams(vmem_limit_bytes=24 * 2**20)


def in_hbm(x):
    return pltpu.with_memory_space_constraint(x, pltpu.HBM)


def cost(flops, size):
    return pl.CostEstimate(flops=flops, bytes_accessed=size, transcendentals=0)


def slots_of(sizes, place, cap, ids_ref, choice_ref):
    experts, hot = sizes[:2]
    top, count = ids_ref.shape
    key = ids_ref[...] + experts * choice_ref[...]
    row = lax.broadcasted_iota(I32, (2 * experts, count), 0)
    hits = [key[k : k + 1] == row for k in range(top)]
    member = functools.reduce(jnp.logical_or, hits)
    later = lax.broadcasted_iota(I32, (count, count), 0) < lax.broadcasted_iota(
        I32, (count, count), 1
    )
    rank = dot(jnp.where(member, 1.0, 0.0).astype(BF16), jnp.where(later, 1.0, 0.0).astype(BF16))
    row_one = lax.broadcasted_iota(I32, (2 * experts, 1), 0)
    limit = jnp.zeros((2 * experts, 1), I32)
    for e in range(experts):
        limit = jnp.where(row_one == e, cap[e], limit)
    for j in range(hot):
        limit = jnp.where(row_one == place[0, j] + experts, cap[experts + j], limit)
    kept = member & (rank < limit.astype(F32))
    return jnp.where(kept, rank, -1.0), hits


def columns_of(sizes, place, chunk):
    experts, hot, _, half, room_a, room_b, direct = sizes
    per = room_a + room_b
    columns = len(chunk) * per
    column = lax.broadcasted_iota(I32, (1, columns), 1)
    block = jnp.floor((column.astype(F32) + 0.5) * (1.0 / per)).astype(I32)
    slot = column - block * per
    if direct:
        flip = jnp.zeros((1, columns), I32)
        for i, j in enumerate(chunk):
            flip = jnp.where(block == i, j, flip)
        dest = flip ^ lax.axis_index("expert")
    else:
        dest = block + chunk[0]
    pair_key = jnp.full((1, columns), -1, I32)
    start = jnp.zeros((1, columns), I32)
    for j in range(hot):
        owner, host = dest == place[0, j], dest == place[1, j]
        pair_key = jnp.where(owner | host, place[0, j] + experts, pair_key)
        start = jnp.where(host, half, start)
    first = slot < room_a
    in_pair = slot - room_a
    wanted = jnp.where(first, dest, jnp.where(in_pair < half, pair_key, -1))
    place_rank = jnp.where(first, slot, in_pair + start).astype(F32)
    place_rank = jnp.where(wanted >= 0, place_rank, -2.0)
    spread = jnp.where(
        lax.broadcasted_iota(I32, (2 * experts, columns), 0) == wanted, 1.0, 0.0
    )
    return spread, place_rank


def fetch(pairs, sems):
    copies = [
        pltpu.make_async_copy(src, dst, sems.at[i]) for i, (src, dst) in enumerate(pairs)
    ]
    for copy in copies:
        copy.start()
    return copies


def route_kernel(sizes, chunks, place_in, cap_in, ids_in, choice_in, tok_in, *refs):
    pieces = refs[:-6]
    place, cap, ids_ref, choice_ref, tok_ref, sems = refs[-6:]
    copies = fetch(
        (
            (ids_in, ids_ref),
            (choice_in, choice_ref),
            (place_in, place),
            (cap_in, cap),
            (tok_in, tok_ref),
        ),
        sems,
    )
    for copy in copies[:4]:
        copy.wait()
    spread, place_rank = columns_of(sizes, place, sum(chunks, ()))
    replicas = spread.shape[0]
    turned = jnp.concatenate([spread, jnp.broadcast_to(place_rank, (8, place_rank.shape[1]))]).T
    rank, _ = slots_of(sizes, place, cap, ids_ref, choice_ref)
    slot = dot(turned[:, :replicas].astype(BF16), rank.astype(BF16))
    picks = jnp.where(slot == turned[:, replicas : replicas + 1], 1.0, 0.0).astype(BF16)
    copies[4].wait()
    rows = dot(picks, tok_ref[...]).astype(BF16)
    per = pieces[0].shape[0]
    for i, piece in enumerate(pieces):
        piece[...] = rows[i * per : (i + 1) * per]


def weigh_kernel(sizes, chunks, place_in, cap_in, ids_in, choice_in, gate_in, *refs):
    mats = refs[:-6]
    place, cap, ids_ref, choice_ref, gate_ref, sems = refs[-6:]
    copies = fetch(
        (
            (ids_in, ids_ref),
            (choice_in, choice_ref),
            (place_in, place),
            (cap_in, cap),
            (gate_in, gate_ref),
        ),
        sems,
    )
    for copy in copies:
        copy.wait()
    rank, hits = slots_of(sizes, place, cap, ids_ref, choice_ref)
    weight = jnp.zeros(rank.shape, F32)
    for k, hit in enumerate(hits):
        weight = jnp.where(hit, gate_ref[k : k + 1], weight)
    weight, rank = weight.T, rank.T.astype(BF16)
    weight_high = weight.astype(BF16)
    weight_low = (weight - weight_high.astype(F32)).astype(BF16)
    for c, chunk in enumerate(chunks):
        spread, place_rank = columns_of(sizes, place, chunk)
        spread = spread.astype(BF16)
        chosen = dot(rank, spread) == place_rank
        for part, out in zip((weight_high, weight_low), mats[2 * c : 2 * c + 2]):
            out[...] = jnp.where(chosen, dot(part, spread), 0.0).astype(BF16)


def hosting(place):
    found = jnp.int32(0)
    for j in range(place.shape[1]):
        found = jnp.where(place[1, j] == lax.axis_index("expert"), 1, found)
    return found


def stage_weights(place_in, place, sems, moves):
    looked = pltpu.make_async_copy(place_in, place, sems.at[0])
    looked.start()
    copies = []

    def begin(which, i):
        for src, dst in moves(which, i):
            copies.append(pltpu.make_async_copy(src, dst, sems.at[len(copies) + 1]))
            copies[-1].start()

    begin(0, 0)
    looked.wait()
    begin(hosting(place), 1)
    for copy in copies:
        copy.wait()


def stage_kernel(parts, ks, place_in, w_gate, w_up, *refs):
    outs, place, sems = refs[:-2], refs[-2], refs[-1]
    block = outs[0].shape[2] // 2

    def moves(which, i):
        for k, out in zip(ks, outs):
            q = lax.axis_index("dp") ^ role(k, parts, lax.axis_index("expert"))
            columns = pl.ds(pl.multiple_of(q * block, block), block)
            for g, w in enumerate((w_gate, w_up)):
                yield w.at[0, which, :, columns], out.at[i, :, pl.ds(g * block, block)]

    stage_weights(place_in, place, sems, moves)


def stage_down_kernel(parts, place_in, w_down, out, place, sems):
    block = out.shape[1] // parts

    def moves(which, i):
        for k in range(parts):
            q = lax.axis_index("dp") ^ role(k, parts, lax.axis_index("expert"))
            units = pl.ds(pl.multiple_of(q * block, block), block)
            yield w_down.at[0, which, units], out.at[i, pl.ds(k * block, block)]

    stage_weights(place_in, place, sems, moves)


def up_sums(xa, xb, weights, out):
    rows_a = xa.shape[0]
    out[:rows_a] = dot(xa, weights[0]).astype(out.dtype)
    out[rows_a:] = dot(xb, weights[1]).astype(out.dtype)


def up_first_kernel(sizes, *refs):
    blocks, room_a, room_b = sizes
    x_refs, weights = refs[:blocks], refs[blocks]
    out, xa, xb = refs[blocks + 1 :]
    for i, ref in enumerate(x_refs):
        xa[i * room_a : (i + 1) * room_a] = ref[:room_a]
        xb[i * room_b : (i + 1) * room_b] = ref[room_a:]
    up_sums(xa[...], xb[...], weights, out)


def up_next_kernel(xa, xb, weights, out):
    up_sums(xa[...], xb[...], weights, out)


def hidden_kernel(own, *refs):
    out = refs[-1]
    block = own.shape[1] // 2
    total = own[...]
    for ref in refs[:-1]:
        total += ref[...].astype(F32)
    out[...] = (jax.nn.silu(total[:, :block]) * total[:, block:]).astype(BF16)


def down_kernel(sizes, w, *refs):
    parts, blocks, room_a, room_b = sizes
    hids, outs, full = refs[:parts], refs[parts:-1], refs[-1]
    rows_a, depth = blocks * room_a, hids[0].shape[1]
    for k, h in enumerate(hids):
        full[:, k * depth : (k + 1) * depth] = h[...]
    ra = dot(full[:rows_a], w[0]).astype(BF16)
    rb = dot(full[rows_a:], w[1]).astype(BF16)
    for i, out in enumerate(outs):
        out[:room_a] = ra[i * room_a : (i + 1) * room_a]
        out[room_a:] = rb[i * room_b : (i + 1) * room_b]


def combine_kernel(has_base, *refs):
    base, (high, low) = refs[:has_base], refs[has_base : has_base + 2]
    pieces, out, res = refs[has_base + 2 : -2], refs[-2], refs[-1]
    per = pieces[0].shape[0]
    for i, ref in enumerate(pieces):
        res[i * per : (i + 1) * per] = ref[...]
    rows = res[...]
    total = dot(high[...], rows) + dot(low[...], rows)
    for ref in base:
        total += ref[...]
    out[...] = total.astype(out.dtype)


def flips(n, j):
    return [(i, i ^ j) for i in range(n)]


def role(k, parts, expert):
    if parts != 4 or k not in (1, 2):
        return k
    return k + (3 - 2 * k) * (expert % 2)


def to_partner(x, k):
    parts, experts = lax.axis_size("dp"), lax.axis_size("expert")
    pairs = [
        (p * experts + e, (p ^ role(k, parts, e)) * experts + e)
        for p in range(parts)
        for e in range(experts)
    ]
    return lax.ppermute(x, ("dp", "expert"), pairs)


def exchange(pieces, chunks, axis):
    n = len(pieces)
    if n > DIRECT_LIMIT:
        moved = lax.all_to_all(jnp.stack(pieces), axis, split_axis=0, concat_axis=0, tiled=True)
        return [moved[i] for i in range(n)]
    moved = []
    for j, piece in zip([j for chunk in chunks for j in chunk], pieces):
        moved.append(lax.ppermute(piece, axis, flips(n, j)) if j else piece)
    return moved


def chunks_of(experts):
    if experts == 8:
        return ((4, 5, 1, 0), (2, 3, 6, 7))
    return (tuple(range(experts)),)


def on_device(
    tokens, expert_ids, replica_choice, gate_weights, placement, capacity, w_gate, w_up, w_down
):
    experts = lax.axis_size("expert")
    parts = lax.axis_size("dp")
    count, cols = tokens.shape
    ff = w_gate.shape[3]
    hot = placement.shape[0]
    room = slot_room(count, expert_ids.shape[1], experts)
    half = -(-room // 2)
    room_a, room_b = round_up(room, 16), round_up(half, 16)
    per = room_a + room_b
    chunks = chunks_of(experts)
    sds = jax.ShapeDtypeStruct
    hbm = pl.BlockSpec(memory_space=pltpu.HBM)
    top = expert_ids.shape[1]
    sizes = (experts, hot, room, half, room_a, room_b, experts <= DIRECT_LIMIT)
    small = [placement.T, capacity, expert_ids.T, replica_choice.T]
    small_scratch = [
        pltpu.SMEM((2, hot), I32),
        pltpu.SMEM(capacity.shape, I32),
        pltpu.VMEM((top, count), I32),
        pltpu.VMEM((top, count), I32),
    ]
    pieces = pl.pallas_call(
        functools.partial(route_kernel, sizes, chunks),
        out_shape=[sds((per, cols), BF16)] * experts,
        in_specs=[hbm] * 5,
        out_specs=vmem_specs(experts),
        scratch_shapes=small_scratch
        + [pltpu.VMEM((count, cols), BF16), pltpu.SemaphoreType.DMA((5,))],
        compiler_params=PARAMS,
        name="route",
    )(*map(in_hbm, [*small, tokens]))
    mat_shapes = [sds((count, len(c) * per), BF16) for c in chunks for _ in range(2)]
    mats = pl.pallas_call(
        functools.partial(weigh_kernel, sizes, chunks),
        out_shape=mat_shapes,
        in_specs=[hbm] * 5,
        out_specs=vmem_specs(len(mat_shapes)),
        scratch_shapes=small_scratch
        + [pltpu.VMEM((top, count), F32), pltpu.SemaphoreType.DMA((5,))],
        compiler_params=PARAMS,
        name="weigh",
    )(*map(in_hbm, [*small, gate_weights.T]))
    arrived = exchange(pieces, chunks, "expert")

    block = ff // parts
    order = list(range(parts - 1, 0, -1)) + [0]
    staged = {}
    for ks in (order[:-1], [0]):
        made = pl.pallas_call(
            functools.partial(stage_kernel, parts, ks),
            out_shape=[sds((2, cols, 2 * block), BF16)] * len(ks),
            in_specs=[hbm] * 3,
            out_specs=vmem_specs(len(ks)),
            scratch_shapes=[pltpu.SMEM((2, hot), I32), pltpu.SemaphoreType.DMA((4 * len(ks) + 1,))],
            compiler_params=PARAMS,
            cost_estimate=cost(0, 16 * cols * block * len(ks)),
        )(*map(in_hbm, [placement.T, w_gate, w_up]))
        staged.update(zip(ks, made))
    staged_down = pl.pallas_call(
        functools.partial(stage_down_kernel, parts),
        out_shape=sds((2, ff, cols), BF16),
        in_specs=[hbm] * 2,
        out_specs=vmem_specs(1)[0],
        scratch_shapes=[pltpu.SMEM((2, hot), I32), pltpu.SemaphoreType.DMA((2 * parts + 1,))],
        compiler_params=PARAMS,
        cost_estimate=cost(0, 8 * cols * ff),
        name="stage_down",
    )(*map(in_hbm, [placement.T, w_down]))

    results, done = [], 0
    for chunk in chunks:
        blocks = len(chunk)
        rows_a, rows = blocks * room_a, blocks * per
        step = 2 * rows * cols * block
        sums = {}
        for i, k in enumerate(order):
            piece = sds((rows, 2 * block), BF16 if k else F32)
            halves = [sds((rows_a, cols), BF16), sds((rows - rows_a, cols), BF16)]
            made = pl.pallas_call(
                up_next_kernel
                if i
                else functools.partial(up_first_kernel, (blocks, room_a, room_b)),
                out_shape=[piece] + ([] if i else halves),
                in_specs=vmem_specs(3 if i else blocks + 1),
                out_specs=vmem_specs(1 if i else 3),
                compiler_params=PARAMS,
                cost_estimate=cost(2 * step, rows * (cols + 2 * block) * 2),
                name="up",
            )(*([xa, xb] if i else arrived[done : done + blocks]), staged[k])
            sums[k] = made[0]
            if not i:
                xa, xb = made[1:]
            if k:
                sums[k] = to_partner(sums[k], k)
        hidden = pl.pallas_call(
            hidden_kernel,
            out_shape=sds((rows, block), BF16),
            in_specs=vmem_specs(parts),
            out_specs=vmem_specs(1)[0],
            compiler_params=PARAMS,
            name="hidden",
        )(*[sums[k] for k in range(parts)])
        spread = {0: hidden}
        for k in order[:-1]:
            spread[k] = to_partner(hidden, k)
        results += pl.pallas_call(
            functools.partial(down_kernel, (parts, blocks, room_a, room_b)),
            out_shape=[sds((per, cols), BF16)] * blocks,
            in_specs=vmem_specs(1 + parts),
            out_specs=vmem_specs(blocks),
            scratch_shapes=[pltpu.VMEM((rows, ff), BF16)],
            compiler_params=PARAMS,
            cost_estimate=cost(parts * step, 4 * cols * ff),
            name="down",
        )(staged_down, *[spread[k] for k in range(parts)])
        done += blocks
    returned = exchange(results, chunks, "expert")
    total, done = [], 0
    for c, chunk in enumerate(chunks):
        last = c + 1 == len(chunks)
        total = [
            pl.pallas_call(
                functools.partial(combine_kernel, len(total)),
                out_shape=sds((count, cols), BF16 if last else F32),
                in_specs=vmem_specs(len(total) + 2 + len(chunk)),
                out_specs=vmem_specs(1)[0],
                scratch_shapes=[pltpu.VMEM((len(chunk) * per, cols), BF16)],
                compiler_params=PARAMS,
                name="combine",
            )(*total, *mats[2 * c : 2 * c + 2], *returned[done : done + len(chunk)])
        ]
        done += len(chunk)
    return total[0]


def solution(mesh):
    return jax.shard_map(
        on_device,
        mesh=mesh,
        in_specs=(
            P("expert", "dp"),
            P("expert", None),
            P("expert", None),
            P("expert", None),
            P(),
            P(),
            P("expert", None, "dp", None),
            P("expert", None, "dp", None),
            P("expert", None, None, "dp"),
        ),
        out_specs=P("expert", "dp"),
        check_vma=False,
    )
```

```python
import functools

import jax
import jax.numpy as jnp
from jax import lax
from jax.experimental import pallas as pl
from jax.experimental.pallas import tpu as pltpu
from jax.sharding import PartitionSpec as P


BF16 = jnp.bfloat16
F32 = jnp.float32
I32 = jnp.int32
DIRECT_LIMIT = 8


def round_up(n, m):
    return -(-n // m) * m


def slot_room(token_count, top_count, expert_count):
    return max(2, min(token_count // 4, 3 * token_count * top_count // (4 * expert_count)))


def dot(a, b):
    return jnp.dot(a, b, preferred_element_type=F32)


def vmem_specs(n):
    return [pl.BlockSpec(memory_space=pltpu.VMEM)] * n


PARAMS = pltpu.CompilerParams(vmem_limit_bytes=24 * 2**20)


def in_hbm(x):
    return pltpu.with_memory_space_constraint(x, pltpu.HBM)


def cost(flops, size):
    return pl.CostEstimate(flops=flops, bytes_accessed=size, transcendentals=0)


def slots_of(sizes, place, cap, ids_ref, choice_ref):
    experts, hot = sizes[:2]
    top, count = ids_ref.shape
    key = ids_ref[...] + experts * choice_ref[...]
    row = lax.broadcasted_iota(I32, (2 * experts, count), 0)
    hits = [key[k : k + 1] == row for k in range(top)]
    member = functools.reduce(jnp.logical_or, hits)
    later = lax.broadcasted_iota(I32, (count, count), 0) < lax.broadcasted_iota(
        I32, (count, count), 1
    )
    rank = dot(jnp.where(member, 1.0, 0.0).astype(BF16), jnp.where(later, 1.0, 0.0).astype(BF16))
    row_one = lax.broadcasted_iota(I32, (2 * experts, 1), 0)
    limit = jnp.zeros((2 * experts, 1), I32)
    for e in range(experts):
        limit = jnp.where(row_one == e, cap[e], limit)
    for j in range(hot):
        limit = jnp.where(row_one == place[0, j] + experts, cap[experts + j], limit)
    kept = member & (rank < limit.astype(F32))
    return jnp.where(kept, rank, -1.0), hits


def columns_of(sizes, place, chunk):
    experts, hot, _, half, room_a, room_b, direct = sizes
    per = room_a + room_b
    columns = len(chunk) * per
    column = lax.broadcasted_iota(I32, (1, columns), 1)
    block = jnp.floor((column.astype(F32) + 0.5) * (1.0 / per)).astype(I32)
    slot = column - block * per
    if direct:
        flip = jnp.zeros((1, columns), I32)
        for i, j in enumerate(chunk):
            flip = jnp.where(block == i, j, flip)
        dest = flip ^ lax.axis_index("expert")
    else:
        dest = block + chunk[0]
    pair_key = jnp.full((1, columns), -1, I32)
    start = jnp.zeros((1, columns), I32)
    for j in range(hot):
        owner, host = dest == place[0, j], dest == place[1, j]
        pair_key = jnp.where(owner | host, place[0, j] + experts, pair_key)
        start = jnp.where(host, half, start)
    first = slot < room_a
    in_pair = slot - room_a
    wanted = jnp.where(first, dest, jnp.where(in_pair < half, pair_key, -1))
    place_rank = jnp.where(first, slot, in_pair + start).astype(F32)
    place_rank = jnp.where(wanted >= 0, place_rank, -2.0)
    spread = jnp.where(
        lax.broadcasted_iota(I32, (2 * experts, columns), 0) == wanted, 1.0, 0.0
    )
    return spread, place_rank


def fetch(pairs, sems):
    copies = [
        pltpu.make_async_copy(src, dst, sems.at[i]) for i, (src, dst) in enumerate(pairs)
    ]
    for copy in copies:
        copy.start()
    return copies


def route_kernel(sizes, chunks, place_in, cap_in, ids_in, choice_in, tok_in, *refs):
    pieces = refs[:-6]
    place, cap, ids_ref, choice_ref, tok_ref, sems = refs[-6:]
    copies = fetch(
        (
            (ids_in, ids_ref),
            (choice_in, choice_ref),
            (place_in, place),
            (cap_in, cap),
            (tok_in, tok_ref),
        ),
        sems,
    )
    for copy in copies[:4]:
        copy.wait()
    spread, place_rank = columns_of(sizes, place, sum(chunks, ()))
    replicas = spread.shape[0]
    turned = jnp.concatenate([spread, jnp.broadcast_to(place_rank, (8, place_rank.shape[1]))]).T
    rank, _ = slots_of(sizes, place, cap, ids_ref, choice_ref)
    slot = dot(turned[:, :replicas].astype(BF16), rank.astype(BF16))
    picks = jnp.where(slot == turned[:, replicas : replicas + 1], 1.0, 0.0).astype(BF16)
    copies[4].wait()
    rows = dot(picks, tok_ref[...]).astype(BF16)
    per = pieces[0].shape[0]
    for i, piece in enumerate(pieces):
        piece[...] = rows[i * per : (i + 1) * per]


def weigh_kernel(sizes, chunks, place_in, cap_in, ids_in, choice_in, gate_in, *refs):
    mats = refs[:-6]
    place, cap, ids_ref, choice_ref, gate_ref, sems = refs[-6:]
    copies = fetch(
        (
            (ids_in, ids_ref),
            (choice_in, choice_ref),
            (place_in, place),
            (cap_in, cap),
            (gate_in, gate_ref),
        ),
        sems,
    )
    for copy in copies:
        copy.wait()
    rank, hits = slots_of(sizes, place, cap, ids_ref, choice_ref)
    weight = jnp.zeros(rank.shape, F32)
    for k, hit in enumerate(hits):
        weight = jnp.where(hit, gate_ref[k : k + 1], weight)
    weight, rank = weight.T, rank.T.astype(BF16)
    weight_high = weight.astype(BF16)
    weight_low = (weight - weight_high.astype(F32)).astype(BF16)
    for c, chunk in enumerate(chunks):
        spread, place_rank = columns_of(sizes, place, chunk)
        spread = spread.astype(BF16)
        chosen = dot(rank, spread) == place_rank
        for part, out in zip((weight_high, weight_low), mats[2 * c : 2 * c + 2]):
            out[...] = jnp.where(chosen, dot(part, spread), 0.0).astype(BF16)


def hosting(place):
    found = jnp.int32(0)
    for j in range(place.shape[1]):
        found = jnp.where(place[1, j] == lax.axis_index("expert"), 1, found)
    return found


def stage_weights(place_in, place, sems, moves):
    looked = pltpu.make_async_copy(place_in, place, sems.at[0])
    looked.start()
    copies = []

    def begin(which, i):
        for src, dst in moves(which, i):
            copies.append(pltpu.make_async_copy(src, dst, sems.at[len(copies) + 1]))
            copies[-1].start()

    begin(0, 0)
    looked.wait()
    begin(hosting(place), 1)
    for copy in copies:
        copy.wait()


def stage_kernel(parts, ks, place_in, w_gate, w_up, *refs):
    outs, place, sems = refs[:-2], refs[-2], refs[-1]
    block = outs[0].shape[2] // 2

    def moves(which, i):
        for k, out in zip(ks, outs):
            q = lax.axis_index("dp") ^ role(k, parts, lax.axis_index("expert"))
            columns = pl.ds(pl.multiple_of(q * block, block), block)
            for g, w in enumerate((w_gate, w_up)):
                yield w.at[0, which, :, columns], out.at[i, :, pl.ds(g * block, block)]

    stage_weights(place_in, place, sems, moves)


def stage_down_kernel(parts, place_in, w_down, out, place, sems):
    block = out.shape[1] // parts

    def moves(which, i):
        for k in range(parts):
            q = lax.axis_index("dp") ^ role(k, parts, lax.axis_index("expert"))
            units = pl.ds(pl.multiple_of(q * block, block), block)
            yield w_down.at[0, which, units], out.at[i, pl.ds(k * block, block)]

    stage_weights(place_in, place, sems, moves)


def up_sums(xa, xb, weights, out):
    rows_a = xa.shape[0]
    out[:rows_a] = dot(xa, weights[0]).astype(out.dtype)
    out[rows_a:] = dot(xb, weights[1]).astype(out.dtype)


def up_first_kernel(sizes, *refs):
    blocks, room_a, room_b = sizes
    x_refs, weights = refs[:blocks], refs[blocks]
    out, xa, xb = refs[blocks + 1 :]
    for i, ref in enumerate(x_refs):
        xa[i * room_a : (i + 1) * room_a] = ref[:room_a]
        xb[i * room_b : (i + 1) * room_b] = ref[room_a:]
    up_sums(xa[...], xb[...], weights, out)


def up_next_kernel(xa, xb, weights, out):
    up_sums(xa[...], xb[...], weights, out)


def hidden_kernel(own, *refs):
    out = refs[-1]
    block = own.shape[1] // 2
    total = own[...]
    for ref in refs[:-1]:
        total += ref[...].astype(F32)
    out[...] = (jax.nn.silu(total[:, :block]) * total[:, block:]).astype(BF16)


def down_kernel(sizes, w, *refs):
    parts, blocks, room_a, room_b = sizes
    hids, outs, full = refs[:parts], refs[parts:-1], refs[-1]
    rows_a, depth = blocks * room_a, hids[0].shape[1]
    for k, h in enumerate(hids):
        full[:, k * depth : (k + 1) * depth] = h[...]
    ra = dot(full[:rows_a], w[0]).astype(BF16)
    rb = dot(full[rows_a:], w[1]).astype(BF16)
    for i, out in enumerate(outs):
        out[:room_a] = ra[i * room_a : (i + 1) * room_a]
        out[room_a:] = rb[i * room_b : (i + 1) * room_b]


def combine_kernel(has_base, *refs):
    base, (high, low) = refs[:has_base], refs[has_base : has_base + 2]
    pieces, out, res = refs[has_base + 2 : -2], refs[-2], refs[-1]
    per = pieces[0].shape[0]
    for i, ref in enumerate(pieces):
        res[i * per : (i + 1) * per] = ref[...]
    rows = res[...]
    total = dot(high[...], rows) + dot(low[...], rows)
    for ref in base:
        total += ref[...]
    out[...] = total.astype(out.dtype)


def flips(n, j):
    return [(i, i ^ j) for i in range(n)]


def role(k, parts, expert):
    if parts != 4 or k not in (1, 2):
        return k
    return k + (3 - 2 * k) * (expert % 2)


def to_partner(x, k):
    parts, experts = lax.axis_size("dp"), lax.axis_size("expert")
    pairs = [
        (p * experts + e, (p ^ role(k, parts, e)) * experts + e)
        for p in range(parts)
        for e in range(experts)
    ]
    return lax.ppermute(x, ("dp", "expert"), pairs)


def exchange(pieces, chunks, axis):
    n = len(pieces)
    if not direct(n):
        moved = lax.all_to_all(jnp.stack(pieces), axis, split_axis=0, concat_axis=0, tiled=True)
        return [moved[i] for i in range(n)]
    moved = []
    for j, piece in zip([j for chunk in chunks for j in chunk], pieces):
        moved.append(lax.ppermute(piece, axis, flips(n, j)) if j else piece)
    return moved


def direct(experts):
    return experts <= DIRECT_LIMIT and experts & (experts - 1) == 0


def chunks_of(experts):
    if experts < 4 or not direct(experts):
        return (tuple(range(experts)),)
    near = [j for j in range(2, experts) if not j & 2]
    return (tuple(near + [1, 0]), tuple(j for j in range(experts) if j & 2))


def on_device(
    tokens, expert_ids, replica_choice, gate_weights, placement, capacity, w_gate, w_up, w_down
):
    experts = lax.axis_size("expert")
    parts = lax.axis_size("dp")
    count, cols = tokens.shape
    ff = w_gate.shape[3]
    hot = placement.shape[0]
    room = slot_room(count, expert_ids.shape[1], experts)
    half = -(-room // 2)
    room_a, room_b = round_up(room, 16), round_up(half, 16)
    per = room_a + room_b
    chunks = chunks_of(experts)
    sds = jax.ShapeDtypeStruct
    hbm = pl.BlockSpec(memory_space=pltpu.HBM)
    top = expert_ids.shape[1]
    sizes = (experts, hot, room, half, room_a, room_b, direct(experts))
    small = [placement.T, capacity, expert_ids.T, replica_choice.T]
    small_scratch = [
        pltpu.SMEM((2, hot), I32),
        pltpu.SMEM(capacity.shape, I32),
        pltpu.VMEM((top, count), I32),
        pltpu.VMEM((top, count), I32),
    ]
    pieces = pl.pallas_call(
        functools.partial(route_kernel, sizes, chunks),
        out_shape=[sds((per, cols), BF16)] * experts,
        in_specs=[hbm] * 5,
        out_specs=vmem_specs(experts),
        scratch_shapes=small_scratch
        + [pltpu.VMEM((count, cols), BF16), pltpu.SemaphoreType.DMA((5,))],
        compiler_params=PARAMS,
        name="route",
    )(*map(in_hbm, [*small, tokens]))
    mat_shapes = [sds((count, len(c) * per), BF16) for c in chunks for _ in range(2)]
    mats = pl.pallas_call(
        functools.partial(weigh_kernel, sizes, chunks),
        out_shape=mat_shapes,
        in_specs=[hbm] * 5,
        out_specs=vmem_specs(len(mat_shapes)),
        scratch_shapes=small_scratch
        + [pltpu.VMEM((top, count), F32), pltpu.SemaphoreType.DMA((5,))],
        compiler_params=PARAMS,
        name="weigh",
    )(*map(in_hbm, [*small, gate_weights.T]))
    arrived = exchange(pieces, chunks, "expert")

    block = ff // parts
    order = list(range(parts - 1, 0, -1)) + [0]
    staged = {}
    for ks in (order[:-1], [0]):
        made = pl.pallas_call(
            functools.partial(stage_kernel, parts, ks),
            out_shape=[sds((2, cols, 2 * block), BF16)] * len(ks),
            in_specs=[hbm] * 3,
            out_specs=vmem_specs(len(ks)),
            scratch_shapes=[pltpu.SMEM((2, hot), I32), pltpu.SemaphoreType.DMA((4 * len(ks) + 1,))],
            compiler_params=PARAMS,
            cost_estimate=cost(0, 16 * cols * block * len(ks)),
        )(*map(in_hbm, [placement.T, w_gate, w_up]))
        staged.update(zip(ks, made))
    staged_down = pl.pallas_call(
        functools.partial(stage_down_kernel, parts),
        out_shape=sds((2, ff, cols), BF16),
        in_specs=[hbm] * 2,
        out_specs=vmem_specs(1)[0],
        scratch_shapes=[pltpu.SMEM((2, hot), I32), pltpu.SemaphoreType.DMA((2 * parts + 1,))],
        compiler_params=PARAMS,
        cost_estimate=cost(0, 8 * cols * ff),
        name="stage_down",
    )(*map(in_hbm, [placement.T, w_down]))

    results, done = [], 0
    for chunk in chunks:
        blocks = len(chunk)
        rows_a, rows = blocks * room_a, blocks * per
        step = 2 * rows * cols * block
        sums = {}
        for i, k in enumerate(order):
            piece = sds((rows, 2 * block), BF16 if k else F32)
            halves = [sds((rows_a, cols), BF16), sds((rows - rows_a, cols), BF16)]
            made = pl.pallas_call(
                up_next_kernel
                if i
                else functools.partial(up_first_kernel, (blocks, room_a, room_b)),
                out_shape=[piece] + ([] if i else halves),
                in_specs=vmem_specs(3 if i else blocks + 1),
                out_specs=vmem_specs(1 if i else 3),
                compiler_params=PARAMS,
                cost_estimate=cost(2 * step, rows * (cols + 2 * block) * 2),
                name="up",
            )(*([xa, xb] if i else arrived[done : done + blocks]), staged[k])
            sums[k] = made[0]
            if not i:
                xa, xb = made[1:]
            if k:
                sums[k] = to_partner(sums[k], k)
        hidden = pl.pallas_call(
            hidden_kernel,
            out_shape=sds((rows, block), BF16),
            in_specs=vmem_specs(parts),
            out_specs=vmem_specs(1)[0],
            compiler_params=PARAMS,
            name="hidden",
        )(*[sums[k] for k in range(parts)])
        spread = {0: hidden}
        for k in order[:-1]:
            spread[k] = to_partner(hidden, k)
        results += pl.pallas_call(
            functools.partial(down_kernel, (parts, blocks, room_a, room_b)),
            out_shape=[sds((per, cols), BF16)] * blocks,
            in_specs=vmem_specs(1 + parts),
            out_specs=vmem_specs(blocks),
            scratch_shapes=[pltpu.VMEM((rows, ff), BF16)],
            compiler_params=PARAMS,
            cost_estimate=cost(parts * step, 4 * cols * ff),
            name="down",
        )(staged_down, *[spread[k] for k in range(parts)])
        done += blocks
    returned = exchange(results, chunks, "expert")
    total, done = [], 0
    for c, chunk in enumerate(chunks):
        last = c + 1 == len(chunks)
        total = [
            pl.pallas_call(
                functools.partial(combine_kernel, len(total)),
                out_shape=sds((count, cols), BF16 if last else F32),
                in_specs=vmem_specs(len(total) + 2 + len(chunk)),
                out_specs=vmem_specs(1)[0],
                scratch_shapes=[pltpu.VMEM((len(chunk) * per, cols), BF16)],
                compiler_params=PARAMS,
                name="combine",
            )(*total, *mats[2 * c : 2 * c + 2], *returned[done : done + len(chunk)])
        ]
        done += len(chunk)
    return total[0]


def solution(mesh):
    return jax.shard_map(
        on_device,
        mesh=mesh,
        in_specs=(
            P("expert", "dp"),
            P("expert", None),
            P("expert", None),
            P("expert", None),
            P(),
            P(),
            P("expert", None, "dp", None),
            P("expert", None, "dp", None),
            P("expert", None, None, "dp"),
        ),
        out_specs=P("expert", "dp"),
        check_vma=False,
    )
```
